512 devices in a mesh: img: 64 (over z, y), freq: 8 (over x, core).
Axes of the slice: x: 4, y: 8, z: 8, core: 2. Of those that a mesh axis runs over, the one named last changes fastest.
Arguments:
- coef: bfloat16 [16384, 1024], P('img', 'freq'), may hold values from -6 to 6
- neighbours: int32 [50, 16384], P(None, 'img'), may hold values from 0 to 16383, as said below
- rot_bin: int32 [50, 16384], P(None, 'img'), may hold values from 0 to 359
- degree: int32 [16384], P('img'), may hold values from 1 to 50
- v_init: float32 [2, 16384], P(None, 'img'), may hold values from -6 to 6
Outputs:
- vector: float32 [2, 16384], P(None, 'img')
- weights: float32 [50, 16384], P(None, 'img')
The draws below stay inside these ranges and needn't reach their ends.
Inputs may be any that keep to these rules, and one draw needn't show every extreme that they name: `neighbours`: counting devices of 256 consecutive images along img, entry (s, i) names an image on a device at most 8 places from image i's device, cyclically; both distances 8 ahead and behind occur.
All inputs are finite; a program needn't handle non-finite values.
Results may differ from the reference program's by a relative error of at most 0.0004.
Values may be sent and summed in bfloat16 or wider, within the bound.
A program may use at most 64 MiB of HBM per device.

```python
import math
import jax
import jax.numpy as jnp
from jax import lax

FREQS = 64
RADIAL = 8
NEIGH = 50
BINS = 360
ITERS = 3
IMG_DEV = 256
NIMAGES = 16384
SPAN = 8


def draw_neighbours(key, part):
    key_offset, key_local = jax.random.split(jax.random.fold_in(key, 11))
    devices = NIMAGES // IMG_DEV
    offset = jax.random.randint(key_offset, (NEIGH, NIMAGES), -SPAN, SPAN + 1)
    local = jax.random.randint(key_local, (NEIGH, NIMAGES), 0, IMG_DEV)
    column = jnp.arange(NIMAGES)
    first = column % IMG_DEV == 0
    slot = jnp.arange(NEIGH)[:, None]
    offset = jnp.where(first[None, :] & (slot == 0), SPAN, offset)
    offset = jnp.where(first[None, :] & (slot == 1), -SPAN, offset)
    owner = (column[None, :] // IMG_DEV + offset) % devices
    return (owner * IMG_DEV + local).astype(jnp.int32)


def set_ends(values, own_key, low, largest):
    shape = values.shape
    spot = [jax.random.randint(jax.random.fold_in(own_key, axis), (), 0, shape[axis]) for axis in range(len(shape))]
    values = values.at[tuple(spot)].set(low)
    longest = shape.index(max(shape))
    spot[longest] = (spot[longest] + 1) % shape[longest]
    return values.at[tuple(spot)].set(largest)


def levels(own_key, dims, shards, least, largest):
    loudness = 1.0
    for axis_at, blocks in shards:
        steps = jax.random.uniform(jax.random.fold_in(jax.random.fold_in(own_key, 6), axis_at), (blocks,), jnp.float32, least / len(shards), largest / len(shards))
        loudness = loudness * jnp.repeat(jnp.exp(steps), dims[axis_at] // blocks).reshape((-1,) + (1,) * (len(dims) - 1 - axis_at))
    return loudness


def normal_values(stream_key, extent, scale, reach, cuts=(), kind=jnp.bfloat16):
    array = scale * jax.random.normal(stream_key, extent, jnp.float32)
    if cuts:
        array = array * levels(stream_key, extent, cuts, -0.22, 0.18)
    return jnp.clip(array, -reach, reach).astype(kind)


def setup_inputs(seed: int = 0) -> dict:
    arg_keys = jax.random.split(jax.random.key(seed), 6)
    return {
        "coef": normal_values(arg_keys[0], (NIMAGES, 2 * FREQS * RADIAL), 1.0, 6.0, ((0, 64), (1, 8))),
        "neighbours": draw_neighbours(jax.random.fold_in(arg_keys[5], 71), 0),
        "rot_bin": set_ends(jax.random.randint(arg_keys[2], (NEIGH, NIMAGES), 0, BINS), jax.random.fold_in(arg_keys[2], 1), 0, BINS - 1).astype(jnp.int32),
        "degree": set_ends(jax.random.randint(arg_keys[3], (NIMAGES,), 1, NEIGH + 1), jax.random.fold_in(arg_keys[3], 1), 1, NEIGH).astype(jnp.int32),
        "v_init": normal_values(arg_keys[4], (2, NIMAGES), 1.0, 6.0, ((1, 64),), jnp.float32),
    }


def reference(coef, neighbours, rot_bin, degree, v_init):
    own = coef.astype(jnp.float32).reshape(NIMAGES, FREQS, 2, RADIAL)
    own_sq = lax.optimization_barrier(jnp.sum(own * own, axis=(1, 2, 3)))
    freq_index = jnp.arange(FREQS).astype(jnp.float32)

    def one_slot(slot_args):
        index, bins = slot_args
        other = own[index]
        theta = bins.astype(jnp.float32) * (2.0 * math.pi / BINS)
        p_real = lax.optimization_barrier(jnp.sum(own[:, :, 0] * other[:, :, 0] + own[:, :, 1] * other[:, :, 1], axis=-1))
        p_imag = lax.optimization_barrier(jnp.sum(own[:, :, 1] * other[:, :, 0] - own[:, :, 0] * other[:, :, 1], axis=-1))
        angle = theta[:, None] * freq_index[None, :]
        corr = lax.optimization_barrier(jnp.sum(p_real * jnp.cos(angle) - p_imag * jnp.sin(angle), axis=-1))
        return (corr, own_sq[index])
    corr, other_sq = lax.map(one_slot, (neighbours, rot_bin))
    cos_sim = corr * lax.rsqrt(other_sq + 1e-05) * lax.rsqrt(own_sq + 1e-05)[None, :]
    valid = jnp.arange(NEIGH)[:, None] < degree[None, :]
    raw = jnp.where(valid, jnp.exp(64.0 * cos_sim), jnp.float32(0.0))
    weights = raw / lax.optimization_barrier(jnp.sum(raw, axis=0, keepdims=True))
    theta = rot_bin.astype(jnp.float32) * (2.0 * math.pi / BINS)
    cosine = jnp.cos(theta)
    sine = jnp.sin(theta)
    vector = v_init
    for step in range(ITERS):
        part_re = vector[0][neighbours]
        part_im = vector[1][neighbours]
        real = lax.optimization_barrier(jnp.sum(weights * (cosine * part_re - sine * part_im), axis=0))
        imag = lax.optimization_barrier(jnp.sum(weights * (sine * part_re + cosine * part_im), axis=0))
        image = jnp.stack([real, imag])
        total = jnp.sum(image * image)
        vector = image * lax.rsqrt(total / NIMAGES + 1e-06)
    return (vector, weights)
```

```python
import math

import jax
import jax.numpy as jnp
from jax import lax
from jax.experimental import pallas as pl
from jax.experimental.pallas import tpu as pltpu
from jax.sharding import PartitionSpec as P

RADIAL = 8
BINS = 360
ITERS = 3
LANES = 128
SPAN = 8
BLOCKS = 2 * SPAN + 1
PIECE = 24
SQ_ROW = 104

sharpness = 64.0
norm_eps = 1e-05
mean_eps = 1e-06

MESH = pl.DeviceIdType.MESH
STEPS = [sign * dist for dist in range(SPAN, 0, -1) for sign in (1, -1)]


def cos_sin_turns(units):
    turns = jnp.floor((units + 0.5) * (1.0 / BINS))
    rest = units - turns * BINS
    quarter = jnp.floor((rest + 45.0) * (1.0 / 90.0) + 1e-3)
    x = (rest - quarter * 90.0) * (math.pi / 180.0)
    y = x * x
    s = x * (1.0 + y * (-1.0 / 6 + y * (1.0 / 120 + y * (-1.0 / 5040 + y * (1.0 / 362880)))))
    c = 1.0 + y * (-0.5 + y * (1.0 / 24 + y * (-1.0 / 720 + y * (1.0 / 40320))))
    odd = (quarter == 1.0) | (quarter == 3.0)
    cos = jnp.where(odd, s, c)
    sin = jnp.where(odd, c, s)
    cos = jnp.where((quarter == 1.0) | (quarter == 2.0), -cos, cos)
    sin = jnp.where((quarter == 2.0) | (quarter == 3.0), -sin, sin)
    return cos, sin


def img_at(me, step, count):
    return {"img": lax.rem(me + (step + count), count)}


def greet(targets):
    barrier = pltpu.get_barrier_semaphore()
    for target in targets:
        pl.semaphore_signal(barrier, inc=1, device_id=target, device_id_type=MESH)
    pl.semaphore_wait(barrier, len(targets))


def window_kernel(count, coef_ref, vec_ref, win_ref, vwin_ref, send, recv, vsend, vrecv, local):
    me = lax.axis_index("img")
    greet([img_at(me, step, count) for step in STEPS])
    copies = []
    for n, step in enumerate(STEPS):
        slot = SPAN - step
        for src, dst, ss, rs in ((coef_ref, win_ref, send, recv), (vec_ref, vwin_ref, vsend, vrecv)):
            copy = pltpu.make_async_remote_copy(
                src_ref=src, dst_ref=dst.at[slot], send_sem=ss.at[n], recv_sem=rs.at[n],
                device_id=img_at(me, step, count), device_id_type=MESH)
            copy.start()
            copies.append(copy)
    own = pltpu.make_async_copy(coef_ref, win_ref.at[SPAN], local.at[0])
    own_vec = pltpu.make_async_copy(vec_ref, vwin_ref.at[SPAN], local.at[1])
    own.start()
    own_vec.start()
    own.wait()
    own_vec.wait()
    for copy in copies:
        copy.wait()


def window_call(coef, vec, count):
    rows, width = coef.shape
    n = len(STEPS)
    return pl.pallas_call(
        lambda *refs: window_kernel(count, *refs),
        out_shape=(jax.ShapeDtypeStruct((BLOCKS, rows, width), coef.dtype),
                   jax.ShapeDtypeStruct((BLOCKS, 8, LANES), jnp.float32)),
        in_specs=[pl.BlockSpec(memory_space=pltpu.VMEM)] * 2,
        out_specs=(pl.BlockSpec(memory_space=pltpu.VMEM),) * 2,
        scratch_shapes=[pltpu.SemaphoreType.DMA((n,))] * 4 + [pltpu.SemaphoreType.DMA((2,))],
        compiler_params=pltpu.CompilerParams(collective_id=0, has_side_effects=True),
        name="window",
    )(coef, vec)


def split_exact(value):
    high = value.astype(jnp.bfloat16)
    low = (value - high.astype(jnp.float32)).astype(jnp.bfloat16)
    return jnp.concatenate([high, low], axis=1)


def lane_sums(select, value):
    return lax.dot_general(select, value, (((1,), (1,)), ((), ())), preferred_element_type=jnp.float32)


def pair_kernel(slots, idx_ref, win_ref, bins_ref, out_ref, wide, turned, *tiles):
    rows = win_ref.shape[1]
    first = lax.axis_index("freq") * (LANES // (2 * RADIAL))
    lane = lax.broadcasted_iota(jnp.int32, (8, 2 * LANES), 1)
    sub = lax.broadcasted_iota(jnp.int32, (8, 2 * LANES), 0)
    select = jnp.where((lane % LANES) // (2 * RADIAL) == sub, 1.0, 0.0).astype(jnp.bfloat16)
    ones = jnp.ones((8, 2 * LANES), jnp.bfloat16)
    freq = (first + lax.broadcasted_iota(jnp.int32, (8, LANES), 0)).astype(jnp.float32)
    out_ref[...] = jnp.zeros_like(out_ref)

    for block in range(BLOCKS):
        part = win_ref[block].astype(jnp.float32)
        wide[block * rows:(block + 1) * rows, :] = part
        for half in range(rows // LANES):
            piece = part[half * LANES:(half + 1) * LANES]
            at = SQ_ROW + block * 2 + half
            out_ref[at:at + 1, :] = lane_sums(ones, split_exact(piece * piece))[0:1]

    own = wide[SPAN * rows:(SPAN + 1) * rows, :]
    column = lax.broadcasted_iota(jnp.int32, own.shape, 1)
    turned[...] = jnp.where(column % (2 * RADIAL) < RADIAL,
                            pltpu.roll(own, LANES - RADIAL, 1), -pltpu.roll(own, RADIAL, 1))

    per = len(tiles)

    def body(step, carry):
        for n in range(per):
            row = step * per + n
            tile = tiles[n]
            for pair in range(LANES):
                tile[pair:pair + 1, :] = wide[pl.ds(idx_ref[row, pair], 1), :]
        for n in range(per):
            row = step * per + n
            half = n % 2
            other = tiles[n][...]
            base = SPAN * rows + half * LANES
            real = split_exact(wide[base:base + LANES, :] * other)
            imag = split_exact(turned[half * LANES:(half + 1) * LANES, :] * other)
            sums = lane_sums(select, jnp.concatenate([real, imag], axis=0))
            units = bins_ref[pl.ds(row, 1), :].astype(jnp.float32) * freq
            cos, sin = cos_sin_turns(units)
            terms = sums[:, :LANES] * cos - sums[:, LANES:] * sin
            out_ref[pl.ds(row, 1), :] = jnp.sum(terms, axis=0, keepdims=True)
        return carry

    lax.fori_loop(0, 2 * slots // per, body, 0)


def pair_call(idx, window, bins, slots):
    blocks, rows, width = window.shape
    vmem = pl.BlockSpec(memory_space=pltpu.VMEM)
    return pl.pallas_call(
        lambda *refs: pair_kernel(slots, *refs),
        out_shape=jax.ShapeDtypeStruct((8 * PIECE, LANES), jnp.float32),
        in_specs=[pl.BlockSpec(memory_space=pltpu.SMEM), vmem, vmem],
        out_specs=vmem,
        scratch_shapes=[pltpu.VMEM((blocks * rows, width), jnp.float32),
                        pltpu.VMEM((rows, width), jnp.float32)]
        + [pltpu.VMEM((LANES, LANES), jnp.float32)] * 4,
        name="pairs",
    )(idx, window, bins)


def pick(low, high, sources):
    count = len(low)
    found = None
    for row in range(BLOCKS * 2):
        wide = [jnp.broadcast_to(part, (8, LANES)) for part in sources(row)]
        got = [[jnp.take_along_axis(part, low[m], axis=1, mode="promise_in_bounds") for m in range(count)]
               for part in wide]
        if found is None:
            found = got
        else:
            hit = [high[m] == row for m in range(count)]
            found = [[jnp.where(hit[m], new[m], old[m]) for m in range(count)] for new, old in zip(got, found)]
    return found


def fold(total):
    total = total + pltpu.roll(total, 4, 0)
    return total + pltpu.roll(total, 2, 0)


def power_kernel(count, groups, part_ref, vwin_ref, idx_ref, bins_ref, deg_ref, weights_ref, vec_ref,
                 rs_buf, ag_buf, vec1, vec2, ynorm, znorm,
                 rs_send, rs_recv, ag_send, ag_recv, v_send, v_recv, n_send, n_recv):
    me = lax.axis_index("img")
    mine = lax.axis_index("freq")
    y, z = lax.rem(me, 8), me // 8
    freq_at = lambda q: {"freq": lax.rem(mine + q, 8)}
    y_at = lambda q: {"img": z * 8 + lax.rem(y + q, 8)}
    z_at = lambda q: {"img": lax.rem(z + q, 8) * 8 + y}
    greet([img_at(me, step, count) for step in STEPS] + [freq_at(q) for q in range(1, 8)]
          + [y_at(q) for q in range(1, 8)] + [z_at(q) for q in range(1, 8)])

    copies = []
    for q in range(1, 8):
        copy = pltpu.make_async_remote_copy(
            src_ref=part_ref.at[lax.rem(mine + q, 8)], dst_ref=rs_buf.at[q - 1],
            send_sem=rs_send.at[q - 1], recv_sem=rs_recv.at[q - 1], device_id=freq_at(q), device_id_type=MESH)
        copy.start()
        copies.append(copy)
    sub = lax.broadcasted_iota(jnp.int32, (8, LANES), 0)
    low, high, cosine, sine, valid = [], [], [], [], []
    for m in range(groups):
        idx = idx_ref[m * 8:(m + 1) * 8, :]
        low.append(idx & (LANES - 1))
        high.append(idx >> 7)
        cos, sin = cos_sin_turns(bins_ref[m * 8:(m + 1) * 8, :].astype(jnp.float32))
        cosine.append(cos)
        sine.append(sin)
        valid.append((sub // 2 + m * 4) < deg_ref[...])
    for copy in copies:
        copy.wait()
    total = part_ref[mine]
    for q in range(7):
        total = total + rs_buf[q]
    ag_buf[mine] = total
    copies = []
    for q in range(1, 8):
        copy = pltpu.make_async_remote_copy(
            src_ref=ag_buf.at[mine], dst_ref=ag_buf.at[mine],
            send_sem=ag_send.at[q - 1], recv_sem=ag_recv.at[q - 1], device_id=freq_at(q), device_id_type=MESH)
        copy.start()
        copies.append(copy)
    for copy in copies:
        copy.wait()

    def ag_row(row, size):
        piece, at = row // PIECE, row % PIECE
        return ag_buf[piece, at:at + size, :]

    sq_row = lambda row: ag_row(SQ_ROW + row, 1)
    own = jnp.where(sub % 2 == 0, sq_row(2 * SPAN), sq_row(2 * SPAN + 1))
    own_root = lax.rsqrt(own + norm_eps)
    (other_sq,) = pick(low, high, lambda row: (sq_row(row),))
    raw = []
    for m in range(groups):
        cos_sim = ag_row(m * 8, 8) * lax.rsqrt(other_sq[m] + norm_eps) * own_root
        raw.append(jnp.where(valid[m], jnp.exp(sharpness * cos_sim), 0.0))
    denom = raw[0]
    for m in range(1, groups):
        denom = denom + raw[m]
    denom = fold(denom)
    for m in range(groups):
        weight = raw[m] / denom
        weights_ref[m * 8:(m + 1) * 8, :] = weight
        cosine[m] = weight * cosine[m]
        sine[m] = weight * sine[m]

    norms = []
    source = vwin_ref
    for step in range(ITERS):
        here = source
        sources = lambda row: (here[row // 2, row % 2:row % 2 + 1, :], here[row // 2, 2 + row % 2:3 + row % 2, :])
        real_at, imag_at = pick(low, high, sources)
        real = imag = jnp.zeros((8, LANES), jnp.float32)
        for m in range(groups):
            real = real + (cosine[m] * real_at[m] - sine[m] * imag_at[m])
            imag = imag + (sine[m] * real_at[m] + cosine[m] * imag_at[m])
        real, imag = fold(real), fold(imag)
        square = real * real + imag * imag
        norms.append(square + pltpu.roll(square, 1, 0))
        packed = jnp.where(sub % 4 < 2, real, imag)
        if step < ITERS - 1:
            into = (vec1, vec2)[step]
            into[SPAN] = packed
            copies = []
            for n, hop in enumerate(STEPS):
                copy = pltpu.make_async_remote_copy(
                    src_ref=into.at[SPAN], dst_ref=into.at[SPAN - hop], send_sem=v_send.at[step, n],
                    recv_sem=v_recv.at[step, n], device_id=img_at(me, hop, count), device_id_type=MESH)
                copy.start()
                copies.append(copy)
            for copy in copies:
                copy.wait()
            source = into

    message = jnp.where(sub == 0, norms[0], jnp.where(sub == 1, norms[1], norms[2]))
    for axis, (buf, where) in enumerate(((ynorm, y_at), (znorm, z_at))):
        buf[7] = message
        copies = []
        for q in range(1, 8):
            copy = pltpu.make_async_remote_copy(
                src_ref=buf.at[7], dst_ref=buf.at[q - 1], send_sem=n_send.at[axis, q - 1],
                recv_sem=n_recv.at[axis, q - 1], device_id=where(q), device_id_type=MESH)
            copy.start()
            copies.append(copy)
        for copy in copies:
            copy.wait()
        for q in range(7):
            message = message + buf[q]
    sums = jnp.sum(message, axis=1, keepdims=True)
    images = count * 2 * LANES
    scale = lax.rsqrt(sums[0:1] / images + mean_eps)
    for step in range(1, ITERS):
        scale = scale * lax.rsqrt(scale * scale * sums[step:step + 1] / images + mean_eps)
    vec_ref[...] = packed * scale


def power_call(part, vwin, idx, bins, deg, count):
    groups = idx.shape[0] // 8
    vmem = pl.BlockSpec(memory_space=pltpu.VMEM)
    n = len(STEPS)
    dma = pltpu.SemaphoreType.DMA
    return pl.pallas_call(
        lambda *refs: power_kernel(count, groups, *refs),
        out_shape=(jax.ShapeDtypeStruct(idx.shape, jnp.float32), jax.ShapeDtypeStruct((8, LANES), jnp.float32)),
        in_specs=[vmem] * 5,
        out_specs=(vmem, vmem),
        scratch_shapes=[pltpu.VMEM((7, PIECE, LANES), jnp.float32), pltpu.VMEM((8, PIECE, LANES), jnp.float32),
                        pltpu.VMEM((BLOCKS, 8, LANES), jnp.float32), pltpu.VMEM((BLOCKS, 8, LANES), jnp.float32),
                        pltpu.VMEM((8, 8, LANES), jnp.float32), pltpu.VMEM((8, 8, LANES), jnp.float32),
                        dma((7,)), dma((7,)), dma((7,)), dma((7,)), dma((2, n)), dma((2, n)), dma((2, 7)), dma((2, 7))],
        compiler_params=pltpu.CompilerParams(collective_id=1, has_side_effects=True),
        name="power",
    )(part, vwin, idx, bins, deg)


def shards(coef, neighbours, rot_bin, degree, v_init):
    rows = coef.shape[0]
    slots = neighbours.shape[0]
    count = lax.axis_size("img")
    offset = (neighbours // rows - lax.axis_index("img") + SPAN + count) % count
    position = offset * rows + neighbours % rows
    tall = lambda value: jnp.pad(value.reshape(2 * slots, LANES), ((0, SQ_ROW - 2 * slots), (0, 0)))
    idx = tall(position)
    bins = tall(rot_bin)
    deg = jnp.tile(degree.reshape(2, LANES), (4, 1))
    vec = jnp.tile(v_init.reshape(4, LANES), (2, 1))
    window, vwin = window_call(coef, vec, count)
    part = pair_call(idx, window, bins, slots)
    weights, vector = power_call(part.reshape(8, PIECE, LANES), vwin, idx, bins, deg, count)
    return vector[:4].reshape(2, rows), weights[:2 * slots].reshape(slots, rows)


def solution(mesh):
    return jax.shard_map(
        shards,
        mesh=mesh,
        in_specs=(P("img", "freq"), P(None, "img"), P(None, "img"), P("img"), P(None, "img")),
        out_specs=(P(None, "img"), P(None, "img")),
        check_vma=False,
    )
```

```python
import math

import jax
import jax.numpy as jnp
from jax import lax
from jax.experimental import pallas as pl
from jax.experimental.pallas import tpu as pltpu
from jax.sharding import PartitionSpec as P

RADIAL = 8
BINS = 360
ITERS = 3
LANES = 128
SPAN = 8
BLOCKS = 2 * SPAN + 1
PIECE = 24
SQ_ROW = 104
OWN_ROW = SQ_ROW + 2 * BLOCKS

sharpness = 64.0
norm_eps = 1e-05
mean_eps = 1e-06

MESH = pl.DeviceIdType.MESH
STEPS = [sign * dist for dist in range(SPAN, 0, -1) for sign in (1, -1)]


def cos_sin_turns(units):
    turns = jnp.floor((units + 0.5) * (1.0 / BINS))
    rest = units - turns * BINS
    quarter = jnp.floor((rest + 45.0) * (1.0 / 90.0) + 1e-3)
    x = (rest - quarter * 90.0) * (math.pi / 180.0)
    y = x * x
    s = x * (1.0 + y * (-1.0 / 6 + y * (1.0 / 120 + y * (-1.0 / 5040 + y * (1.0 / 362880)))))
    c = 1.0 + y * (-0.5 + y * (1.0 / 24 + y * (-1.0 / 720 + y * (1.0 / 40320))))
    odd = (quarter == 1.0) | (quarter == 3.0)
    cos = jnp.where(odd, s, c)
    sin = jnp.where(odd, c, s)
    cos = jnp.where((quarter == 1.0) | (quarter == 2.0), -cos, cos)
    sin = jnp.where((quarter == 2.0) | (quarter == 3.0), -sin, sin)
    return cos, sin


def img_at(me, step, count):
    return {"img": lax.rem(me + (step + count), count)}


def greet(targets):
    barrier = pltpu.get_barrier_semaphore()
    for target in targets:
        pl.semaphore_signal(barrier, inc=1, device_id=target, device_id_type=MESH)
    pl.semaphore_wait(barrier, len(targets))


def ring(me, mine_z, mine_y):
    y_at = lambda q: {"img": mine_z * 8 + lax.rem(mine_y + q, 8)}
    z_at = lambda q: {"img": lax.rem(mine_z + q, 8) * 8 + mine_y}
    return y_at, z_at


def landing_slot(mine_y, hop):
    if hop == -SPAN:
        return 2 * SPAN
    row = lax.div(mine_y + (hop + SPAN), SPAN) - 1
    return mine_y + SPAN * row * row


def window_kernel(count, coef_ref, nei_ref, bin_ref, v_ref, win_ref, vwin_ref, idx_ref, bins_ref, message,
                  y_send, y_recv, z_send, z_recv, v_send, v_recv, local):
    me = lax.axis_index("img")
    y, z = lax.rem(me, 8), lax.div(me, 8)
    y_at, z_at = ring(me, z, y)
    message[...] = jnp.zeros_like(message)
    for part in range(2):
        for half in range(2):
            message[part * 2 + half:part * 2 + half + 1, :] = v_ref[part:part + 1, half * LANES:(half + 1) * LANES]
    greet([img_at(me, step, count) for step in STEPS])
    started = []

    def send(src, dst, ss, rs, target):
        copy = pltpu.make_async_remote_copy(
            src_ref=src, dst_ref=dst, send_sem=ss, recv_sem=rs, device_id=target, device_id_type=MESH)
        copy.start()
        return copy

    ways = (1, 7)
    flows = [[send(coef_ref, win_ref.at[y], y_send.at[w, 0], y_recv.at[w, 0], y_at(ways[w]))] for w in range(2)]
    rows = [send(coef_ref, win_ref.at[8 + y], z_send.at[7], z_recv.at[7], z_at(1)),
            send(coef_ref, win_ref.at[16], z_send.at[8], z_recv.at[8], z_at(7))]
    own = pltpu.make_async_copy(coef_ref, win_ref.at[y], local.at[0])
    own.start()
    small = [send(message, vwin_ref.at[landing_slot(y, step)], v_send.at[n], v_recv.at[n], img_at(me, step, count))
             for n, step in enumerate(STEPS)]
    vwin_ref[y] = message[...]

    slots = nei_ref.shape[0]
    nei = nei_ref[...]
    block = nei >> 8
    hop = ((block - me + (SPAN + count)) & (count - 1)) - SPAN
    slot = jnp.where(hop == SPAN, 2 * SPAN, (block & 7) + jnp.where((block >> 3) != z, SPAN, 0))
    place = slot * (2 * LANES) + (nei & (2 * LANES - 1))
    for half in range(2):
        idx_ref[pl.ds(half, slots, stride=2), :] = place[:, half * LANES:(half + 1) * LANES]
        bins_ref[pl.ds(half, slots, stride=2), :] = bin_ref[:, half * LANES:(half + 1) * LANES]
    idx_ref[2 * slots:, :] = jnp.zeros((SQ_ROW - 2 * slots, LANES), jnp.int32)
    bins_ref[2 * slots:, :] = jnp.zeros((SQ_ROW - 2 * slots, LANES), jnp.int32)

    for q in range(1, 4):
        for w in range(2):
            from_block = lax.rem(y + (8 - q if w == 0 else q), 8)
            turn = lax.div(y - q + 8, 8) if w == 0 else lax.div(y + q, 8)
            flows[w][q - 1].wait_recv()
            held = win_ref.at[from_block]
            if q == 3:
                span = pl.ds(w * LANES, LANES)
                src = win_ref.at[from_block, span]
            else:
                src = held
            flows[w].append(send(src, src, y_send.at[w, q], y_recv.at[w, q], y_at(ways[w])))
            at = (q - 1) * 2 + w
            rows.append(send(held, win_ref.at[8 + from_block], z_send.at[at], z_recv.at[at], z_at(1 + 6 * turn)))
    for w in range(2):
        flows[w][3].wait_recv()
    far = lax.rem(y + 4, 8)
    rows.append(send(win_ref.at[far], win_ref.at[8 + far], z_send.at[6], z_recv.at[6], z_at(1 + 6 * lax.div(y + 4, 8))))
    for copy in rows:
        copy.wait_recv()
    for copy in rows + flows[0] + flows[1]:
        copy.wait_send()
    for copy in small:
        copy.wait()
    own.wait()


def window_call(coef, neighbours, rot_bin, v_init, count):
    rows, width = coef.shape
    n = len(STEPS)
    vmem = pl.BlockSpec(memory_space=pltpu.VMEM)
    dma = pltpu.SemaphoreType.DMA
    return pl.pallas_call(
        lambda *refs: window_kernel(count, *refs),
        out_shape=(jax.ShapeDtypeStruct((BLOCKS, rows, width), coef.dtype),
                   jax.ShapeDtypeStruct((BLOCKS, 8, LANES), jnp.float32),
                   jax.ShapeDtypeStruct((SQ_ROW, LANES), jnp.int32),
                   jax.ShapeDtypeStruct((SQ_ROW, LANES), jnp.int32)),
        in_specs=[vmem] * 4,
        out_specs=(vmem,) * 4,
        scratch_shapes=[pltpu.VMEM((8, LANES), jnp.float32), dma((2, 4)), dma((2, 4)), dma((9,)), dma((9,)),
                        dma((n,)), dma((n,)), dma((1,))],
        compiler_params=pltpu.CompilerParams(collective_id=0, has_side_effects=True),
        name="window",
    )(coef, neighbours, rot_bin, v_init)


def split_exact(value):
    high = value.astype(jnp.bfloat16)
    low = (value - high.astype(jnp.float32)).astype(jnp.bfloat16)
    return jnp.concatenate([high, low], axis=1)


def lane_sums(select, value):
    return lax.dot_general(select, value, (((1,), (1,)), ((), ())), preferred_element_type=jnp.float32)


def pair_kernel(slots, idx_ref, win_ref, bins_ref, out_ref, wide, own_tile, turned, *tiles):
    rows = win_ref.shape[1]
    first = lax.axis_index("freq") * (LANES // (2 * RADIAL))
    lane = lax.broadcasted_iota(jnp.int32, (8, 2 * LANES), 1)
    sub = lax.broadcasted_iota(jnp.int32, (8, 2 * LANES), 0)
    select = jnp.where((lane % LANES) // (2 * RADIAL) == sub, 1.0, 0.0).astype(jnp.bfloat16)
    ones = jnp.ones((8, 2 * LANES), jnp.bfloat16)
    freq = (first + lax.broadcasted_iota(jnp.int32, (8, LANES), 0)).astype(jnp.float32)
    out_ref[...] = jnp.zeros_like(out_ref)

    for block in range(BLOCKS):
        part = win_ref[block].astype(jnp.float32)
        wide[block * rows:(block + 1) * rows, :] = part
        for half in range(rows // LANES):
            piece = part[half * LANES:(half + 1) * LANES]
            at = SQ_ROW + block * 2 + half
            out_ref[at:at + 1, :] = lane_sums(ones, split_exact(piece * piece))[0:1]

    slot = lax.rem(lax.axis_index("img"), 8)
    own = win_ref[slot].astype(jnp.float32)
    own_tile[...] = own
    for half in range(rows // LANES):
        piece = own[half * LANES:(half + 1) * LANES]
        at = OWN_ROW + half
        out_ref[at:at + 1, :] = lane_sums(ones, split_exact(piece * piece))[0:1]
    column = lax.broadcasted_iota(jnp.int32, own.shape, 1)
    turned[...] = jnp.where(column % (2 * RADIAL) < RADIAL,
                            pltpu.roll(own, LANES - RADIAL, 1), -pltpu.roll(own, RADIAL, 1))

    per = len(tiles)

    def body(step, carry):
        for n in range(per):
            row = step * per + n
            tile = tiles[n]
            for pair in range(LANES):
                tile[pair:pair + 1, :] = wide[pl.ds(idx_ref[row, pair], 1), :]
        for n in range(per):
            row = step * per + n
            half = n % 2
            other = tiles[n][...]
            real = split_exact(own_tile[half * LANES:(half + 1) * LANES, :] * other)
            imag = split_exact(turned[half * LANES:(half + 1) * LANES, :] * other)
            sums = lane_sums(select, jnp.concatenate([real, imag], axis=0))
            units = bins_ref[pl.ds(row, 1), :].astype(jnp.float32) * freq
            cos, sin = cos_sin_turns(units)
            terms = sums[:, :LANES] * cos - sums[:, LANES:] * sin
            out_ref[pl.ds(row, 1), :] = jnp.sum(terms, axis=0, keepdims=True)
        return carry

    lax.fori_loop(0, 2 * slots // per, body, 0)


def pair_call(idx, window, bins, slots):
    blocks, rows, width = window.shape
    vmem = pl.BlockSpec(memory_space=pltpu.VMEM)
    return pl.pallas_call(
        lambda *refs: pair_kernel(slots, *refs),
        out_shape=jax.ShapeDtypeStruct((8 * PIECE, LANES), jnp.float32),
        in_specs=[pl.BlockSpec(memory_space=pltpu.SMEM), vmem, vmem],
        out_specs=vmem,
        scratch_shapes=[pltpu.VMEM((blocks * rows, width), jnp.float32),
                        pltpu.VMEM((rows, width), jnp.float32), pltpu.VMEM((rows, width), jnp.float32)]
        + [pltpu.VMEM((LANES, LANES), jnp.float32)] * 4,
        name="pairs",
    )(idx, window, bins)


def pick(low, high, sources):
    count = len(low)
    found = None
    for row in range(BLOCKS * 2):
        wide = [jnp.broadcast_to(part, (8, LANES)) for part in sources(row)]
        got = [[jnp.take_along_axis(part, low[m], axis=1, mode="promise_in_bounds") for m in range(count)]
               for part in wide]
        if found is None:
            found = got
        else:
            hit = [high[m] == row for m in range(count)]
            found = [[jnp.where(hit[m], new[m], old[m]) for m in range(count)] for new, old in zip(got, found)]
    return found


def fold(total):
    total = total + pltpu.roll(total, 4, 0)
    return total + pltpu.roll(total, 2, 0)


def power_kernel(count, groups, part_ref, vwin_ref, idx_ref, bins_ref, deg_ref, weights_ref, vec_ref,
                 wbuf, rs_buf, ag_buf, vec1, vec2, ynorm, znorm,
                 rs_send, rs_recv, ag_send, ag_recv, v_send, v_recv, n_send, n_recv):
    me = lax.axis_index("img")
    mine = lax.axis_index("freq")
    y, z = lax.rem(me, 8), lax.div(me, 8)
    freq_at = lambda q: {"freq": lax.rem(mine + q, 8)}
    y_at, z_at = ring(me, z, y)
    greet([img_at(me, step, count) for step in STEPS] + [freq_at(q) for q in range(1, 8)]
          + [y_at(q) for q in range(1, 8)] + [z_at(q) for q in range(1, 8)])

    copies = []
    for q in range(1, 8):
        copy = pltpu.make_async_remote_copy(
            src_ref=part_ref.at[lax.rem(mine + q, 8)], dst_ref=rs_buf.at[q - 1],
            send_sem=rs_send.at[q - 1], recv_sem=rs_recv.at[q - 1], device_id=freq_at(q), device_id_type=MESH)
        copy.start()
        copies.append(copy)
    sub = lax.broadcasted_iota(jnp.int32, (8, LANES), 0)
    degree = jnp.where(sub % 2 == 0, deg_ref[0:1, :], deg_ref[1:2, :])
    low, high, cosine, sine, valid = [], [], [], [], []
    for m in range(groups):
        idx = idx_ref[m * 8:(m + 1) * 8, :]
        low.append(idx & (LANES - 1))
        high.append(idx >> 7)
        cos, sin = cos_sin_turns(bins_ref[m * 8:(m + 1) * 8, :].astype(jnp.float32))
        cosine.append(cos)
        sine.append(sin)
        valid.append((sub // 2 + m * 4) < degree)
    for copy in copies:
        copy.wait()
    total = part_ref[mine]
    for q in range(7):
        total = total + rs_buf[q]
    ag_buf[mine] = total
    copies = []
    for q in range(1, 8):
        copy = pltpu.make_async_remote_copy(
            src_ref=ag_buf.at[mine], dst_ref=ag_buf.at[mine],
            send_sem=ag_send.at[q - 1], recv_sem=ag_recv.at[q - 1], device_id=freq_at(q), device_id_type=MESH)
        copy.start()
        copies.append(copy)
    for copy in copies:
        copy.wait()

    def ag_row(row, size):
        piece, at = row // PIECE, row % PIECE
        return ag_buf[piece, at:at + size, :]

    sq_row = lambda row: ag_row(SQ_ROW + row, 1)
    own = jnp.where(sub % 2 == 0, ag_row(OWN_ROW, 1), ag_row(OWN_ROW + 1, 1))
    own_root = lax.rsqrt(own + norm_eps)
    (other_sq,) = pick(low, high, lambda row: (sq_row(row),))
    raw = []
    for m in range(groups):
        cos_sim = ag_row(m * 8, 8) * lax.rsqrt(other_sq[m] + norm_eps) * own_root
        raw.append(jnp.where(valid[m], jnp.exp(sharpness * cos_sim), 0.0))
    denom = raw[0]
    for m in range(1, groups):
        denom = denom + raw[m]
    denom = fold(denom)
    for m in range(groups):
        weight = raw[m] / denom
        wbuf[m * 8:(m + 1) * 8, :] = weight
        cosine[m] = weight * cosine[m]
        sine[m] = weight * sine[m]

    slots = weights_ref.shape[0]
    for half in range(2):
        weights_ref[:, half * LANES:(half + 1) * LANES] = wbuf[pl.ds(half, slots, stride=2), :]

    norms = []
    source = vwin_ref
    for step in range(ITERS):
        here = source
        sources = lambda row: (here[row // 2, row % 2:row % 2 + 1, :], here[row // 2, 2 + row % 2:3 + row % 2, :])
        real_at, imag_at = pick(low, high, sources)
        real = imag = jnp.zeros((8, LANES), jnp.float32)
        for m in range(groups):
            real = real + (cosine[m] * real_at[m] - sine[m] * imag_at[m])
            imag = imag + (sine[m] * real_at[m] + cosine[m] * imag_at[m])
        real, imag = fold(real), fold(imag)
        square = real * real + imag * imag
        norms.append(square + pltpu.roll(square, 1, 0))
        packed = jnp.where(sub % 4 < 2, real, imag)
        if step < ITERS - 1:
            into = (vec1, vec2)[step]
            into[y] = packed
            copies = []
            for n, hop in enumerate(STEPS):
                copy = pltpu.make_async_remote_copy(
                    src_ref=into.at[y], dst_ref=into.at[landing_slot(y, hop)], send_sem=v_send.at[step, n],
                    recv_sem=v_recv.at[step, n], device_id=img_at(me, hop, count), device_id_type=MESH)
                copy.start()
                copies.append(copy)
            for copy in copies:
                copy.wait()
            source = into

    message = jnp.where(sub == 0, norms[0], jnp.where(sub == 1, norms[1], norms[2]))
    for axis, (buf, where) in enumerate(((ynorm, y_at), (znorm, z_at))):
        buf[7] = message
        copies = []
        for q in range(1, 8):
            copy = pltpu.make_async_remote_copy(
                src_ref=buf.at[7], dst_ref=buf.at[q - 1], send_sem=n_send.at[axis, q - 1],
                recv_sem=n_recv.at[axis, q - 1], device_id=where(q), device_id_type=MESH)
            copy.start()
            copies.append(copy)
        for copy in copies:
            copy.wait()
        for q in range(7):
            message = message + buf[q]
    sums = jnp.sum(message, axis=1, keepdims=True)
    images = count * 2 * LANES
    scale = lax.rsqrt(sums[0:1] / images + mean_eps)
    for step in range(1, ITERS):
        scale = scale * lax.rsqrt(scale * scale * sums[step:step + 1] / images + mean_eps)
    vector = packed * scale
    for part in range(2):
        for half in range(2):
            row = part * 2 + half
            vec_ref[part:part + 1, half * LANES:(half + 1) * LANES] = vector[row:row + 1, :]


def power_call(part, vwin, idx, bins, deg, count, slots):
    groups = idx.shape[0] // 8
    vmem = pl.BlockSpec(memory_space=pltpu.VMEM)
    n = len(STEPS)
    dma = pltpu.SemaphoreType.DMA
    return pl.pallas_call(
        lambda *refs: power_kernel(count, groups, *refs),
        out_shape=(jax.ShapeDtypeStruct((slots, 2 * LANES), jnp.float32), jax.ShapeDtypeStruct((2, 2 * LANES), jnp.float32)),
        in_specs=[vmem] * 5,
        out_specs=(vmem, vmem),
        scratch_shapes=[pltpu.VMEM(idx.shape, jnp.float32), pltpu.VMEM((7, PIECE, LANES), jnp.float32), pltpu.VMEM((8, PIECE, LANES), jnp.float32),
                        pltpu.VMEM((BLOCKS, 8, LANES), jnp.float32), pltpu.VMEM((BLOCKS, 8, LANES), jnp.float32),
                        pltpu.VMEM((8, 8, LANES), jnp.float32), pltpu.VMEM((8, 8, LANES), jnp.float32),
                        dma((7,)), dma((7,)), dma((7,)), dma((7,)), dma((2, n)), dma((2, n)), dma((2, 7)), dma((2, 7))],
        compiler_params=pltpu.CompilerParams(collective_id=1, has_side_effects=True),
        name="power",
    )(part, vwin, idx, bins, deg)


def shards(coef, neighbours, rot_bin, degree, v_init):
    slots = neighbours.shape[0]
    count = lax.axis_size("img")
    window, vwin, idx, bins = window_call(coef, neighbours, rot_bin, v_init, count)
    part = pair_call(idx, window, bins, slots)
    weights, vector = power_call(
        part.reshape(8, PIECE, LANES), vwin, idx, bins, degree.reshape(2, LANES), count, slots)
    return vector, weights


def solution(mesh):
    return jax.shard_map(
        shards,
        mesh=mesh,
        in_specs=(P("img", "freq"), P(None, "img"), P(None, "img"), P("img"), P(None, "img")),
        out_specs=(P(None, "img"), P(None, "img")),
        check_vma=False,
    )
```

```python
import math

import jax
import jax.numpy as jnp
from jax import lax
from jax.experimental import pallas as pl
from jax.experimental.pallas import tpu as pltpu
from jax.sharding import PartitionSpec as P

RADIAL = 8
BINS = 360
ITERS = 3
LANES = 128
SPAN = 8
BLOCKS = 2 * SPAN + 1
PIECE = 16
TALL = 104

sharpness = 64.0
norm_eps = 1e-05
mean_eps = 1e-06

MESH = pl.DeviceIdType.MESH
STEPS = [sign * dist for dist in range(SPAN, 0, -1) for sign in (1, -1)]


def cos_sin_turns(units):
    turns = jnp.floor((units + 0.5) * (1.0 / BINS))
    rest = units - turns * BINS
    quarter = jnp.floor((rest + 45.0) * (1.0 / 90.0) + 1e-3)
    x = (rest - quarter * 90.0) * (math.pi / 180.0)
    y = x * x
    s = x * (1.0 + y * (-1.0 / 6 + y * (1.0 / 120 + y * (-1.0 / 5040 + y * (1.0 / 362880)))))
    c = 1.0 + y * (-0.5 + y * (1.0 / 24 + y * (-1.0 / 720 + y * (1.0 / 40320))))
    odd = (quarter == 1.0) | (quarter == 3.0)
    cos = jnp.where(odd, s, c)
    sin = jnp.where(odd, c, s)
    cos = jnp.where((quarter == 1.0) | (quarter == 2.0), -cos, cos)
    sin = jnp.where((quarter == 2.0) | (quarter == 3.0), -sin, sin)
    return cos, sin


def img_at(me, step, count):
    return {"img": lax.rem(me + (step + count), count)}


def greet(targets):
    barrier = pltpu.get_barrier_semaphore()
    for target in targets:
        pl.semaphore_signal(barrier, inc=1, device_id=target, device_id_type=MESH)
    return lambda: pl.semaphore_wait(barrier, len(targets))


def ring(me, mine_z, mine_y):
    y_at = lambda q: {"img": mine_z * 8 + lax.rem(mine_y + q, 8)}
    z_at = lambda q: {"img": lax.rem(mine_z + q, 8) * 8 + mine_y}
    return y_at, z_at


def landing_slot(mine_y, hop):
    if hop == -SPAN:
        return 2 * SPAN
    row = lax.div(mine_y + (hop + SPAN), SPAN) - 1
    return mine_y + SPAN * row * row


def window_kernel(count, coef_ref, nei_ref, bin_ref, v_ref, win_ref, vwin_ref, idx_ref, bins_ref, message, squares,
                  y_send, y_recv, z_send, z_recv, v_send, v_recv, s_send, s_recv, local):
    me = lax.axis_index("img")
    mine = lax.axis_index("freq")
    y, z = lax.rem(me, 8), lax.div(me, 8)
    y_at, z_at = ring(me, z, y)
    freq_at = lambda q: {"freq": lax.rem(mine + q, 8)}
    met = greet([img_at(me, step, count) for step in STEPS] + [freq_at(q) for q in range(1, 8)])
    own = pltpu.make_async_copy(coef_ref, win_ref.at[y], local.at[0])
    own.start()
    ones = jnp.ones((8, 2 * LANES), jnp.bfloat16)
    for half in range(2):
        piece = coef_ref[half * LANES:(half + 1) * LANES, :].astype(jnp.float32)
        sums = lane_sums(ones, split_exact(piece * piece))
        if half == 0:
            first_sums = sums
    sub = lax.broadcasted_iota(jnp.int32, (8, LANES), 0)
    squares[mine] = jnp.where(sub % 2 == 0, first_sums, sums)
    met()

    def send(src, dst, ss, rs, target):
        copy = pltpu.make_async_remote_copy(
            src_ref=src, dst_ref=dst, send_sem=ss, recv_sem=rs, device_id=target, device_id_type=MESH)
        copy.start()
        return copy

    ways = (1, 7)
    chunk = lambda c: pl.ds(c * LANES, LANES)
    flows, rows = {}, []
    for c in range(2):
        for w in range(2):
            flows[w, 0, c] = send(coef_ref.at[chunk(c)], win_ref.at[y, chunk(c)], y_send.at[w, 0, c],
                                  y_recv.at[w, 0, c], y_at(ways[w]))
    for c in range(2):
        rows.append(send(coef_ref.at[chunk(c)], win_ref.at[8 + y, chunk(c)], z_send.at[7, c], z_recv.at[7, c], z_at(1)))
        rows.append(send(coef_ref.at[chunk(c)], win_ref.at[16, chunk(c)], z_send.at[8, c], z_recv.at[8, c], z_at(7)))
    sums = [send(squares.at[mine], squares.at[mine], s_send.at[q - 1], s_recv.at[q - 1], freq_at(q))
            for q in range(1, 8)]

    slots = nei_ref.shape[0]
    nei = nei_ref[...]
    block = nei >> 8
    hop = ((block - me + (SPAN + count)) & (count - 1)) - SPAN
    slot = jnp.where(hop == SPAN, 2 * SPAN, (block & 7) + jnp.where((block >> 3) != z, SPAN, 0))
    place = slot * (2 * LANES) + (nei & (2 * LANES - 1))
    for half in range(2):
        idx_ref[pl.ds(half, slots, stride=2), :] = place[:, half * LANES:(half + 1) * LANES]
        bins_ref[pl.ds(half, slots, stride=2), :] = bin_ref[:, half * LANES:(half + 1) * LANES]
    idx_ref[2 * slots:, :] = jnp.zeros((TALL - 2 * slots, LANES), jnp.int32)
    bins_ref[2 * slots:, :] = jnp.zeros((TALL - 2 * slots, LANES), jnp.int32)

    small = []
    for q in range(1, 5):
        for c in range(2):
            for w in range(2):
                if q == 4 and w != c:
                    continue
                block_at = lax.rem(y + (8 - q if w == 0 else q), 8)
                turn = lax.div(y - q + 8, 8) if w == 0 else lax.div(y + q, 8)
                if q == 4:
                    turn = lax.div(y + 4, 8)
                flows[w, q - 1, c].wait_recv()
                held = win_ref.at[block_at, chunk(c)]
                if q < 3 or (q == 3 and w == c):
                    flows[w, q, c] = send(held, held, y_send.at[w, q, c], y_recv.at[w, q, c], y_at(ways[w]))
                at = (q - 1) * 2 + w if q < 4 else 6
                rows.append(send(held, win_ref.at[8 + block_at, chunk(c)], z_send.at[at, c], z_recv.at[at, c],
                                 z_at(1 + 6 * turn)))
        if q == 1:
            for copy in sums:
                copy.wait()
            total = squares[0]
            for other in range(1, 8):
                total = total + squares[other]
            packed = total
            for part in range(2):
                for half in range(2):
                    value = v_ref[part:part + 1, half * LANES:(half + 1) * LANES]
                    packed = jnp.where(sub == part * 2 + half, value, packed)
            message[...] = packed
            vwin_ref[y] = packed
            small = [send(message, vwin_ref.at[landing_slot(y, step)], v_send.at[n], v_recv.at[n],
                          img_at(me, step, count)) for n, step in enumerate(STEPS)]
    for copy in small + rows:
        copy.wait()
    for copy in flows.values():
        copy.wait_send()
    own.wait()


def window_call(coef, neighbours, rot_bin, v_init, count):
    rows, width = coef.shape
    n = len(STEPS)
    vmem = pl.BlockSpec(memory_space=pltpu.VMEM)
    dma = pltpu.SemaphoreType.DMA
    return pl.pallas_call(
        lambda *refs: window_kernel(count, *refs),
        out_shape=(jax.ShapeDtypeStruct((BLOCKS, rows, width), coef.dtype),
                   jax.ShapeDtypeStruct((BLOCKS, 8, LANES), jnp.float32),
                   jax.ShapeDtypeStruct((TALL, LANES), jnp.int32),
                   jax.ShapeDtypeStruct((TALL, LANES), jnp.int32)),
        in_specs=[vmem] * 4,
        out_specs=(vmem,) * 4,
        scratch_shapes=[pltpu.VMEM((8, LANES), jnp.float32), pltpu.VMEM((8, 8, LANES), jnp.float32),
                        dma((2, 4, 2)), dma((2, 4, 2)), dma((9, 2)), dma((9, 2)),
                        dma((n,)), dma((n,)), dma((7,)), dma((7,)), dma((1,))],
        compiler_params=pltpu.CompilerParams(collective_id=0, has_side_effects=True),
        name="window",
    )(coef, neighbours, rot_bin, v_init)


def split_exact(value):
    high = value.astype(jnp.bfloat16)
    low = (value - high.astype(jnp.float32)).astype(jnp.bfloat16)
    return jnp.concatenate([high, low], axis=1)


def lane_sums(select, value):
    return lax.dot_general(select, value, (((1,), (1,)), ((), ())), preferred_element_type=jnp.float32)


def pair_kernel(slots, idx_ref, win_ref, bins_ref, out_ref, wide, own_tile, turned, *tiles):
    rows = win_ref.shape[1]
    first = lax.axis_index("freq") * (LANES // (2 * RADIAL))
    lane = lax.broadcasted_iota(jnp.int32, (8, 2 * LANES), 1)
    sub = lax.broadcasted_iota(jnp.int32, (8, 2 * LANES), 0)
    select = jnp.where((lane % LANES) // (2 * RADIAL) == sub, 1.0, 0.0).astype(jnp.bfloat16)
    freq = (first + lax.broadcasted_iota(jnp.int32, (8, LANES), 0)).astype(jnp.float32)
    out_ref[...] = jnp.zeros_like(out_ref)

    for block in range(BLOCKS):
        wide[block * rows:(block + 1) * rows, :] = win_ref[block].astype(jnp.float32)

    slot = lax.rem(lax.axis_index("img"), 8)
    own = win_ref[slot].astype(jnp.float32)
    own_tile[...] = own
    column = lax.broadcasted_iota(jnp.int32, own.shape, 1)
    turned[...] = jnp.where(column % (2 * RADIAL) < RADIAL,
                            pltpu.roll(own, LANES - RADIAL, 1), -pltpu.roll(own, RADIAL, 1))

    per = len(tiles)

    def body(step, carry):
        for n in range(per):
            row = step * per + n
            tile = tiles[n]
            for pair in range(LANES):
                tile[pair:pair + 1, :] = wide[pl.ds(idx_ref[row, pair], 1), :]
        for n in range(per):
            row = step * per + n
            half = n % 2
            other = tiles[n][...]
            real = split_exact(own_tile[half * LANES:(half + 1) * LANES, :] * other)
            imag = split_exact(turned[half * LANES:(half + 1) * LANES, :] * other)
            sums = lane_sums(select, jnp.concatenate([real, imag], axis=0))
            units = bins_ref[pl.ds(row, 1), :].astype(jnp.float32) * freq
            cos, sin = cos_sin_turns(units)
            terms = sums[:, :LANES] * cos - sums[:, LANES:] * sin
            out_ref[pl.ds(row, 1), :] = jnp.sum(terms, axis=0, keepdims=True)
        return carry

    lax.fori_loop(0, 2 * slots // per, body, 0)


def pair_call(idx, window, bins, slots):
    blocks, rows, width = window.shape
    vmem = pl.BlockSpec(memory_space=pltpu.VMEM)
    return pl.pallas_call(
        lambda *refs: pair_kernel(slots, *refs),
        out_shape=jax.ShapeDtypeStruct((8 * PIECE, LANES), jnp.float32),
        in_specs=[pl.BlockSpec(memory_space=pltpu.SMEM), vmem, vmem],
        out_specs=vmem,
        scratch_shapes=[pltpu.VMEM((blocks * rows, width), jnp.float32),
                        pltpu.VMEM((rows, width), jnp.float32), pltpu.VMEM((rows, width), jnp.float32)]
        + [pltpu.VMEM((LANES, LANES), jnp.float32)] * 4,
        name="pairs",
    )(idx, window, bins)


def pick(low, high, ref, lines):
    found = []
    for where, at in zip(low, high):
        got = [None] * len(lines)
        for row in range(BLOCKS * 2):
            hit = at == row
            for n, line in enumerate(lines):
                first = line + row % 2
                wide = jnp.broadcast_to(ref[row // 2, first:first + 1, :], (8, LANES))
                new = jnp.take_along_axis(wide, where, axis=1, mode="promise_in_bounds")
                got[n] = new if row == 0 else jnp.where(hit, new, got[n])
        found.append(got)
    return found


def fold(total):
    total = total + pltpu.roll(total, 4, 0)
    return total + pltpu.roll(total, 2, 0)


def power_kernel(count, groups, part_ref, vwin_ref, idx_ref, bins_ref, deg_ref, weights_ref, vec_ref,
                 cos_buf, sin_buf, real_buf, imag_buf, root_buf, rs_buf, ag_buf, vec1, vec2, ynorm, znorm,
                 rs_send, rs_recv, ag_send, ag_recv, v_send, v_recv, n_send, n_recv):
    me = lax.axis_index("img")
    mine = lax.axis_index("freq")
    y, z = lax.rem(me, 8), lax.div(me, 8)
    freq_at = lambda q: {"freq": lax.rem(mine + q, 8)}
    y_at, z_at = ring(me, z, y)
    met = greet([img_at(me, step, count) for step in STEPS] + [freq_at(q) for q in range(1, 8)]
                + [y_at(q) for q in range(1, 8)] + [z_at(q) for q in range(1, 8)])
    sub = lax.broadcasted_iota(jnp.int32, (8, LANES), 0)
    degree = jnp.where(sub % 2 == 0, deg_ref[0:1, :], deg_ref[1:2, :])
    low = [idx_ref[m * 8:(m + 1) * 8, :] & (LANES - 1) for m in range(groups)]
    high = [idx_ref[m * 8:(m + 1) * 8, :] >> 7 for m in range(groups)]
    own_sq = vwin_ref[y]
    own_root = lax.rsqrt(jnp.where(sub % 2 == 0, own_sq[4:5], own_sq[5:6]) + norm_eps)
    for m, (real, imag, square) in enumerate(pick(low, high, vwin_ref, (0, 2, 4))):
        cos, sin = cos_sin_turns(bins_ref[m * 8:(m + 1) * 8, :].astype(jnp.float32))
        cos_buf[m] = cos
        sin_buf[m] = sin
        real_buf[m] = cos * real - sin * imag
        imag_buf[m] = sin * real + cos * imag
        root_buf[m] = lax.rsqrt(square + norm_eps) * own_root
    met()

    copies = []
    for q in range(1, 8):
        copy = pltpu.make_async_remote_copy(
            src_ref=part_ref.at[lax.rem(mine + q, 8)], dst_ref=rs_buf.at[q - 1],
            send_sem=rs_send.at[q - 1], recv_sem=rs_recv.at[q - 1], device_id=freq_at(q), device_id_type=MESH)
        copy.start()
        copies.append(copy)
    for copy in copies:
        copy.wait()
    total = part_ref[mine]
    for q in range(7):
        total = total + rs_buf[q]
    ag_buf[mine] = total
    copies = []
    for q in range(1, 8):
        copy = pltpu.make_async_remote_copy(
            src_ref=ag_buf.at[mine], dst_ref=ag_buf.at[mine],
            send_sem=ag_send.at[q - 1], recv_sem=ag_recv.at[q - 1], device_id=freq_at(q), device_id_type=MESH)
        copy.start()
        copies.append(copy)
    for copy in copies:
        copy.wait()

    def ag_row(row, size):
        piece, at = row // PIECE, row % PIECE
        return ag_buf[piece, at:at + size, :]

    denom = jnp.zeros((8, LANES), jnp.float32)
    for m in range(groups):
        cos_sim = ag_row(m * 8, 8) * root_buf[m]
        raw = jnp.where((sub // 2 + m * 4) < degree, jnp.exp(sharpness * cos_sim), 0.0)
        weights_ref[m * 8:(m + 1) * 8, :] = raw
        denom = denom + raw
    share = 1.0 / fold(denom)
    for m in range(groups):
        weights_ref[m * 8:(m + 1) * 8, :] = weights_ref[m * 8:(m + 1) * 8, :] * share

    norms = []
    source = None
    for step in range(ITERS):
        real = imag = jnp.zeros((8, LANES), jnp.float32)
        picked = pick(low, high, source, (0, 2)) if step else [None] * groups
        for m, at in enumerate(picked):
            weight = weights_ref[m * 8:(m + 1) * 8, :]
            if step:
                real_at, imag_at = at
                real = real + weight * (cos_buf[m] * real_at - sin_buf[m] * imag_at)
                imag = imag + weight * (sin_buf[m] * real_at + cos_buf[m] * imag_at)
            else:
                real = real + weight * real_buf[m]
                imag = imag + weight * imag_buf[m]
        real, imag = fold(real), fold(imag)
        square = real * real + imag * imag
        norms.append(square + pltpu.roll(square, 1, 0))
        packed = jnp.where(sub % 4 < 2, real, imag)
        if step < ITERS - 1:
            into = (vec1, vec2)[step]
            into[y] = packed
            copies = []
            for n, hop in enumerate(STEPS):
                copy = pltpu.make_async_remote_copy(
                    src_ref=into.at[y], dst_ref=into.at[landing_slot(y, hop)], send_sem=v_send.at[step, n],
                    recv_sem=v_recv.at[step, n], device_id=img_at(me, hop, count), device_id_type=MESH)
                copy.start()
                copies.append(copy)
            for copy in copies:
                copy.wait()
            source = into

    message = jnp.where(sub == 0, norms[0], jnp.where(sub == 1, norms[1], norms[2]))
    for axis, (buf, where) in enumerate(((ynorm, y_at), (znorm, z_at))):
        buf[7] = message
        copies = []
        for q in range(1, 8):
            copy = pltpu.make_async_remote_copy(
                src_ref=buf.at[7], dst_ref=buf.at[q - 1], send_sem=n_send.at[axis, q - 1],
                recv_sem=n_recv.at[axis, q - 1], device_id=where(q), device_id_type=MESH)
            copy.start()
            copies.append(copy)
        for copy in copies:
            copy.wait()
        for q in range(7):
            message = message + buf[q]
    sums = jnp.sum(message, axis=1, keepdims=True)
    images = count * 2 * LANES
    scale = lax.rsqrt(sums[0:1] / images + mean_eps)
    for step in range(1, ITERS):
        scale = scale * lax.rsqrt(scale * scale * sums[step:step + 1] / images + mean_eps)
    vec_ref[...] = packed * scale


def finish_kernel(tall_ref, packed_ref, weights_ref, vec_ref):
    slots = weights_ref.shape[0]
    for half in range(2):
        lanes = slice(half * LANES, (half + 1) * LANES)
        weights_ref[:, lanes] = tall_ref[pl.ds(half, slots, stride=2), :]
        for part in range(2):
            vec_ref[part:part + 1, lanes] = packed_ref[part * 2 + half:part * 2 + half + 1, :]


def power_call(part, vwin, idx, bins, deg, count):
    groups = idx.shape[0] // 8
    vmem = pl.BlockSpec(memory_space=pltpu.VMEM)
    n = len(STEPS)
    dma = pltpu.SemaphoreType.DMA
    return pl.pallas_call(
        lambda *refs: power_kernel(count, groups, *refs),
        out_shape=(jax.ShapeDtypeStruct(idx.shape, jnp.float32), jax.ShapeDtypeStruct((8, LANES), jnp.float32)),
        in_specs=[vmem] * 5,
        out_specs=(vmem, vmem),
        scratch_shapes=[pltpu.VMEM((groups, 8, LANES), jnp.float32)] * 5 + [pltpu.VMEM((7, PIECE, LANES), jnp.float32), pltpu.VMEM((8, PIECE, LANES), jnp.float32),
                        pltpu.VMEM((BLOCKS, 8, LANES), jnp.float32), pltpu.VMEM((BLOCKS, 8, LANES), jnp.float32),
                        pltpu.VMEM((8, 8, LANES), jnp.float32), pltpu.VMEM((8, 8, LANES), jnp.float32),
                        dma((7,)), dma((7,)), dma((7,)), dma((7,)), dma((2, n)), dma((2, n)), dma((2, 7)), dma((2, 7))],
        compiler_params=pltpu.CompilerParams(collective_id=1, has_side_effects=True),
        name="power",
    )(part, vwin, idx, bins, deg)


def shards(coef, neighbours, rot_bin, degree, v_init):
    slots = neighbours.shape[0]
    count = lax.axis_size("img")
    window, vwin, idx, bins = window_call(coef, neighbours, rot_bin, v_init, count)
    part = pair_call(idx, window, bins, slots)
    tall, packed = power_call(part.reshape(8, PIECE, LANES), vwin, idx, bins, degree.reshape(2, LANES), count)
    vmem = pl.BlockSpec(memory_space=pltpu.VMEM)
    weights, vector = pl.pallas_call(
        finish_kernel,
        out_shape=(jax.ShapeDtypeStruct(neighbours.shape, jnp.float32), jax.ShapeDtypeStruct(v_init.shape, jnp.float32)),
        in_specs=[vmem] * 2,
        out_specs=(vmem, vmem),
        name="finish",
    )(tall, packed)
    return vector, weights


def solution(mesh):
    return jax.shard_map(
        shards,
        mesh=mesh,
        in_specs=(P("img", "freq"), P(None, "img"), P(None, "img"), P("img"), P(None, "img")),
        out_specs=(P(None, "img"), P(None, "img")),
        check_vma=False,
    )
```

```python
import math

import jax
import jax.numpy as jnp
from jax import lax
from jax.experimental import pallas as pl
from jax.experimental.pallas import tpu as pltpu
from jax.sharding import PartitionSpec as P

RADIAL = 8
BINS = 360
ITERS = 3
LANES = 128
SPAN = 8
BLOCKS = 2 * SPAN + 1
PIECE = 16
TALL = 104

sharpness = 64.0
norm_eps = 1e-05
mean_eps = 1e-06

MESH = pl.DeviceIdType.MESH
STEPS = [sign * dist for dist in range(SPAN, 0, -1) for sign in (1, -1)]


def cos_sin_turns(units):
    turns = jnp.floor((units + 0.5) * (1.0 / BINS))
    rest = units - turns * BINS
    quarter = jnp.floor((rest + 45.0) * (1.0 / 90.0) + 1e-3)
    x = (rest - quarter * 90.0) * (math.pi / 180.0)
    y = x * x
    s = x * (1.0 + y * (-1.0 / 6 + y * (1.0 / 120 + y * (-1.0 / 5040 + y * (1.0 / 362880)))))
    c = 1.0 + y * (-0.5 + y * (1.0 / 24 + y * (-1.0 / 720 + y * (1.0 / 40320))))
    odd = (quarter == 1.0) | (quarter == 3.0)
    cos = jnp.where(odd, s, c)
    sin = jnp.where(odd, c, s)
    cos = jnp.where((quarter == 1.0) | (quarter == 2.0), -cos, cos)
    sin = jnp.where((quarter == 2.0) | (quarter == 3.0), -sin, sin)
    return cos, sin


def img_at(me, step, count):
    return {"img": lax.rem(me + (step + count), count)}


def greet(targets):
    barrier = pltpu.get_barrier_semaphore()
    for target in targets:
        pl.semaphore_signal(barrier, inc=1, device_id=target, device_id_type=MESH)
    return lambda: pl.semaphore_wait(barrier, len(targets))


def ring(me, mine_z, mine_y):
    y_at = lambda q: {"img": mine_z * 8 + lax.rem(mine_y + q, 8)}
    z_at = lambda q: {"img": lax.rem(mine_z + q, 8) * 8 + mine_y}
    return y_at, z_at


def landing_slot(mine_y, hop):
    if hop == -SPAN:
        return 2 * SPAN
    row = lax.div(mine_y + (hop + SPAN), SPAN) - 1
    return mine_y + SPAN * row * row


def window_kernel(count, coef_ref, nei_ref, bin_ref, v_ref, win_ref, vwin_ref, idx_ref, bins_ref, message, squares,
                  y_send, y_recv, z_send, z_recv, v_send, v_recv, s_send, s_recv, local):
    me = lax.axis_index("img")
    mine = lax.axis_index("freq")
    y, z = lax.rem(me, 8), lax.div(me, 8)
    y_at, z_at = ring(me, z, y)
    freq_at = lambda q: {"freq": lax.rem(mine + q, 8)}
    met = greet([img_at(me, step, count) for step in STEPS] + [freq_at(q) for q in range(1, 8)])
    own = pltpu.make_async_copy(coef_ref, win_ref.at[y], local.at[0])
    own.start()
    ones = jnp.ones((8, 2 * LANES), jnp.bfloat16)
    for half in range(2):
        piece = coef_ref[half * LANES:(half + 1) * LANES, :].astype(jnp.float32)
        sums = lane_sums(ones, split_exact(piece * piece))
        if half == 0:
            first_sums = sums
    sub = lax.broadcasted_iota(jnp.int32, (8, LANES), 0)
    squares[mine] = jnp.where(sub % 2 == 0, first_sums, sums)
    met()

    def send(src, dst, ss, rs, target):
        copy = pltpu.make_async_remote_copy(
            src_ref=src, dst_ref=dst, send_sem=ss, recv_sem=rs, device_id=target, device_id_type=MESH)
        copy.start()
        return copy

    ways = (1, 7)
    chunk = lambda c: pl.ds(c * LANES, LANES)
    flows, rows = {}, []
    for c in range(2):
        for w in range(2):
            flows[w, 0, c] = send(coef_ref.at[chunk(c)], win_ref.at[y, chunk(c)], y_send.at[w, 0, c],
                                  y_recv.at[w, 0, c], y_at(ways[w]))
    for c in range(2):
        rows.append(send(coef_ref.at[chunk(c)], win_ref.at[8 + y, chunk(c)], z_send.at[7, c], z_recv.at[7, c], z_at(1)))
        rows.append(send(coef_ref.at[chunk(c)], win_ref.at[16, chunk(c)], z_send.at[8, c], z_recv.at[8, c], z_at(7)))
    sums = [send(squares.at[mine], squares.at[mine], s_send.at[q - 1], s_recv.at[q - 1], freq_at(q))
            for q in range(1, 8)]

    slots = nei_ref.shape[0]
    nei = nei_ref[...]
    block = nei >> 8
    hop = ((block - me + (SPAN + count)) & (count - 1)) - SPAN
    slot = jnp.where(hop == SPAN, 2 * SPAN, (block & 7) + jnp.where((block >> 3) != z, SPAN, 0))
    place = slot * (2 * LANES) + (nei & (2 * LANES - 1))
    for half in range(2):
        idx_ref[pl.ds(half, slots, stride=2), :] = place[:, half * LANES:(half + 1) * LANES]
        bins_ref[pl.ds(half, slots, stride=2), :] = bin_ref[:, half * LANES:(half + 1) * LANES]
    idx_ref[2 * slots:, :] = jnp.zeros((TALL - 2 * slots, LANES), jnp.int32)
    bins_ref[2 * slots:, :] = jnp.zeros((TALL - 2 * slots, LANES), jnp.int32)

    small = []
    for q in range(1, 5):
        for c in range(2):
            for w in range(2):
                if q == 4 and w != c:
                    continue
                block_at = lax.rem(y + (8 - q if w == 0 else q), 8)
                turn = lax.div(y - q + 8, 8) if w == 0 else lax.div(y + q, 8)
                if q == 4:
                    turn = lax.div(y + 4, 8)
                flows[w, q - 1, c].wait_recv()
                held = win_ref.at[block_at, chunk(c)]
                if q < 3 or (q == 3 and w == c):
                    flows[w, q, c] = send(held, held, y_send.at[w, q, c], y_recv.at[w, q, c], y_at(ways[w]))
                at = (q - 1) * 2 + w if q < 4 else 6
                rows.append(send(held, win_ref.at[8 + block_at, chunk(c)], z_send.at[at, c], z_recv.at[at, c],
                                 z_at(1 + 6 * turn)))
        if q == 1:
            for copy in sums:
                copy.wait()
            total = squares[0]
            for other in range(1, 8):
                total = total + squares[other]
            packed = total
            for part in range(2):
                for half in range(2):
                    value = v_ref[part:part + 1, half * LANES:(half + 1) * LANES]
                    packed = jnp.where(sub == part * 2 + half, value, packed)
            message[...] = packed
            vwin_ref[y] = packed
            small = [send(message, vwin_ref.at[landing_slot(y, step)], v_send.at[n], v_recv.at[n],
                          img_at(me, step, count)) for n, step in enumerate(STEPS)]
    for copy in small + rows:
        copy.wait()
    for copy in flows.values():
        copy.wait_send()
    own.wait()


def window_call(coef, neighbours, rot_bin, v_init, count):
    rows, width = coef.shape
    n = len(STEPS)
    vmem = pl.BlockSpec(memory_space=pltpu.VMEM)
    dma = pltpu.SemaphoreType.DMA
    return pl.pallas_call(
        lambda *refs: window_kernel(count, *refs),
        out_shape=(jax.ShapeDtypeStruct((BLOCKS, rows, width), coef.dtype),
                   jax.ShapeDtypeStruct((BLOCKS, 8, LANES), jnp.float32),
                   jax.ShapeDtypeStruct((TALL, LANES), jnp.int32),
                   jax.ShapeDtypeStruct((TALL, LANES), jnp.int32)),
        in_specs=[vmem] * 4,
        out_specs=(vmem,) * 4,
        scratch_shapes=[pltpu.VMEM((8, LANES), jnp.float32), pltpu.VMEM((8, 8, LANES), jnp.float32),
                        dma((2, 4, 2)), dma((2, 4, 2)), dma((9, 2)), dma((9, 2)),
                        dma((n,)), dma((n,)), dma((7,)), dma((7,)), dma((1,))],
        compiler_params=pltpu.CompilerParams(collective_id=0, has_side_effects=True),
        name="window",
    )(coef, neighbours, rot_bin, v_init)


def split_exact(value):
    high = value.astype(jnp.bfloat16)
    low = (value - high.astype(jnp.float32)).astype(jnp.bfloat16)
    return jnp.concatenate([high, low], axis=1)


def lane_sums(select, value):
    return lax.dot_general(select, value, (((1,), (1,)), ((), ())), preferred_element_type=jnp.float32)


def pair_kernel(groups, idx_ref, win_ref, bins_ref, out_ref, wide, own_tile, turned, places, arrived, *tiles):
    rows = win_ref.shape[1]
    fetch = lambda group, at: pltpu.make_async_copy(idx_ref.at[group], places[at], arrived.at[at])
    fetch(0, 0).start()
    fetch(1, 1).start()
    first = lax.axis_index("freq") * (LANES // (2 * RADIAL))
    lane = lax.broadcasted_iota(jnp.int32, (8, 2 * LANES), 1)
    sub = lax.broadcasted_iota(jnp.int32, (8, 2 * LANES), 0)
    select = jnp.where((lane % LANES) // (2 * RADIAL) == sub, 1.0, 0.0).astype(jnp.bfloat16)
    freq = (first + lax.broadcasted_iota(jnp.int32, (8, LANES), 0)).astype(jnp.float32)
    line = lax.broadcasted_iota(jnp.int32, (8, LANES), 0)

    for block in range(BLOCKS):
        wide[block * rows:(block + 1) * rows, :] = win_ref[block].astype(jnp.float32)
    own = win_ref[lax.rem(lax.axis_index("img"), 8)].astype(jnp.float32)
    own_tile[...] = own
    column = lax.broadcasted_iota(jnp.int32, own.shape, 1)
    turned[...] = jnp.where(column % (2 * RADIAL) < RADIAL,
                            pltpu.roll(own, LANES - RADIAL, 1), -pltpu.roll(own, RADIAL, 1))
    for group in range(groups, 16):
        out_ref[group] = jnp.zeros((8, LANES), jnp.float32)

    def one_group(group, at, then=None):
        fetch(group, at).wait()
        place = places[at]
        for n in range(8):
            for pair in range(LANES):
                tiles[n][pair:pair + 1, :] = wide[pl.ds(place[n, pair], 1), :]
        if then is not None:
            fetch(then, at).start()
        result = jnp.zeros((8, LANES), jnp.float32)
        for n in range(8):
            half = slice((n % 2) * LANES, (n % 2 + 1) * LANES)
            other = tiles[n][...]
            real = split_exact(own_tile[half, :] * other)
            imag = split_exact(turned[half, :] * other)
            sums = lane_sums(select, jnp.concatenate([real, imag], axis=0))
            units = bins_ref[group, n:n + 1, :].astype(jnp.float32) * freq
            cos, sin = cos_sin_turns(units)
            terms = sums[:, :LANES] * cos - sums[:, LANES:] * sin
            result = jnp.where(line == n, jnp.sum(terms, axis=0, keepdims=True), result)
        out_ref[group] = result

    def body(step, carry):
        one_group(2 * step, 0, 2 * step + 2)
        one_group(2 * step + 1, 1, jnp.minimum(2 * step + 3, groups - 1))
        return carry

    lax.fori_loop(0, groups // 2, body, 0)
    one_group(groups - 1, 0)
    fetch(groups - 1, 1).wait()


def pair_call(idx, window, bins):
    blocks, rows, width = window.shape
    groups = idx.shape[0]
    vmem = pl.BlockSpec(memory_space=pltpu.VMEM)
    return pl.pallas_call(
        lambda *refs: pair_kernel(groups, *refs[:7], refs[7:9], *refs[9:]),
        out_shape=jax.ShapeDtypeStruct((16, 8, LANES), jnp.float32),
        in_specs=[pl.BlockSpec(memory_space=pl.ANY), vmem, vmem],
        out_specs=vmem,
        scratch_shapes=[pltpu.VMEM((blocks * rows, width), jnp.float32),
                        pltpu.VMEM((rows, width), jnp.float32), pltpu.VMEM((rows, width), jnp.float32),
                        pltpu.SMEM((8, LANES), jnp.int32), pltpu.SMEM((8, LANES), jnp.int32),
                        pltpu.SemaphoreType.DMA((2,))]
        + [pltpu.VMEM((LANES, LANES), jnp.float32)] * 8,
        name="pairs",
    )(idx, window, bins)


def pick(low, high, ref, lines):
    found = []
    for where, at in zip(low, high):
        got = [None] * len(lines)
        for row in range(BLOCKS * 2):
            hit = at == row
            for n, line in enumerate(lines):
                first = line + row % 2
                wide = jnp.broadcast_to(ref[row // 2, first:first + 1, :], (8, LANES))
                new = jnp.take_along_axis(wide, where, axis=1, mode="promise_in_bounds")
                got[n] = new if row == 0 else jnp.where(hit, new, got[n])
        found.append(got)
    return found


def fold(total):
    total = total + pltpu.roll(total, 4, 0)
    return total + pltpu.roll(total, 2, 0)


def power_kernel(count, groups, part_ref, vwin_ref, idx_ref, bins_ref, deg_ref, weights_ref, vec_ref,
                 cos_buf, sin_buf, real_buf, imag_buf, root_buf, rs_buf, ag_buf, vec1, vec2, ynorm, znorm,
                 rs_send, rs_recv, ag_send, ag_recv, v_send, v_recv, n_send, n_recv):
    me = lax.axis_index("img")
    mine = lax.axis_index("freq")
    y, z = lax.rem(me, 8), lax.div(me, 8)
    freq_at = lambda q: {"freq": lax.rem(mine + q, 8)}
    y_at, z_at = ring(me, z, y)
    met = greet([img_at(me, step, count) for step in STEPS] + [freq_at(q) for q in range(1, 8)]
                + [y_at(q) for q in range(1, 8)] + [z_at(q) for q in range(1, 8)])
    sub = lax.broadcasted_iota(jnp.int32, (8, LANES), 0)
    degree = jnp.where(sub % 2 == 0, deg_ref[0:1, :], deg_ref[1:2, :])
    low = [idx_ref[m * 8:(m + 1) * 8, :] & (LANES - 1) for m in range(groups)]
    high = [idx_ref[m * 8:(m + 1) * 8, :] >> 7 for m in range(groups)]
    own_sq = vwin_ref[y]
    own_root = lax.rsqrt(jnp.where(sub % 2 == 0, own_sq[4:5], own_sq[5:6]) + norm_eps)
    for m, (real, imag, square) in enumerate(pick(low, high, vwin_ref, (0, 2, 4))):
        cos, sin = cos_sin_turns(bins_ref[m * 8:(m + 1) * 8, :].astype(jnp.float32))
        cos_buf[m] = cos
        sin_buf[m] = sin
        real_buf[m] = cos * real - sin * imag
        imag_buf[m] = sin * real + cos * imag
        root_buf[m] = lax.rsqrt(square + norm_eps) * own_root
    met()

    copies = []
    for q in range(1, 8):
        copy = pltpu.make_async_remote_copy(
            src_ref=part_ref.at[lax.rem(mine + q, 8)], dst_ref=rs_buf.at[q - 1],
            send_sem=rs_send.at[q - 1], recv_sem=rs_recv.at[q - 1], device_id=freq_at(q), device_id_type=MESH)
        copy.start()
        copies.append(copy)
    for copy in copies:
        copy.wait()
    total = part_ref[mine]
    for q in range(7):
        total = total + rs_buf[q]
    ag_buf[mine] = total
    copies = []
    for q in range(1, 8):
        copy = pltpu.make_async_remote_copy(
            src_ref=ag_buf.at[mine], dst_ref=ag_buf.at[mine],
            send_sem=ag_send.at[q - 1], recv_sem=ag_recv.at[q - 1], device_id=freq_at(q), device_id_type=MESH)
        copy.start()
        copies.append(copy)
    for copy in copies:
        copy.wait()

    def ag_row(row, size):
        piece, at = row // PIECE, row % PIECE
        return ag_buf[piece, at:at + size, :]

    denom = jnp.zeros((8, LANES), jnp.float32)
    for m in range(groups):
        cos_sim = ag_row(m * 8, 8) * root_buf[m]
        raw = jnp.where((sub // 2 + m * 4) < degree, jnp.exp(sharpness * cos_sim), 0.0)
        weights_ref[m * 8:(m + 1) * 8, :] = raw
        denom = denom + raw
    share = 1.0 / fold(denom)
    for m in range(groups):
        weights_ref[m * 8:(m + 1) * 8, :] = weights_ref[m * 8:(m + 1) * 8, :] * share

    norms = []
    source = None
    for step in range(ITERS):
        real = imag = jnp.zeros((8, LANES), jnp.float32)
        picked = pick(low, high, source, (0, 2)) if step else [None] * groups
        for m, at in enumerate(picked):
            weight = weights_ref[m * 8:(m + 1) * 8, :]
            if step:
                real_at, imag_at = at
                real = real + weight * (cos_buf[m] * real_at - sin_buf[m] * imag_at)
                imag = imag + weight * (sin_buf[m] * real_at + cos_buf[m] * imag_at)
            else:
                real = real + weight * real_buf[m]
                imag = imag + weight * imag_buf[m]
        real, imag = fold(real), fold(imag)
        square = real * real + imag * imag
        norms.append(square + pltpu.roll(square, 1, 0))
        packed = jnp.where(sub % 4 < 2, real, imag)
        if step < ITERS - 1:
            into = (vec1, vec2)[step]
            into[y] = packed
            copies = []
            for n, hop in enumerate(STEPS):
                copy = pltpu.make_async_remote_copy(
                    src_ref=into.at[y], dst_ref=into.at[landing_slot(y, hop)], send_sem=v_send.at[step, n],
                    recv_sem=v_recv.at[step, n], device_id=img_at(me, hop, count), device_id_type=MESH)
                copy.start()
                copies.append(copy)
            for copy in copies:
                copy.wait()
            source = into

    message = jnp.where(sub == 0, norms[0], jnp.where(sub == 1, norms[1], norms[2]))
    for axis, (buf, where) in enumerate(((ynorm, y_at), (znorm, z_at))):
        buf[7] = message
        copies = []
        for q in range(1, 8):
            copy = pltpu.make_async_remote_copy(
                src_ref=buf.at[7], dst_ref=buf.at[q - 1], send_sem=n_send.at[axis, q - 1],
                recv_sem=n_recv.at[axis, q - 1], device_id=where(q), device_id_type=MESH)
            copy.start()
            copies.append(copy)
        for copy in copies:
            copy.wait()
        for q in range(7):
            message = message + buf[q]
    sums = jnp.sum(message, axis=1, keepdims=True)
    images = count * 2 * LANES
    scale = lax.rsqrt(sums[0:1] / images + mean_eps)
    for step in range(1, ITERS):
        scale = scale * lax.rsqrt(scale * scale * sums[step:step + 1] / images + mean_eps)
    vec_ref[...] = packed * scale


def finish_kernel(tall_ref, packed_ref, weights_ref, vec_ref):
    slots = weights_ref.shape[0]
    for half in range(2):
        lanes = slice(half * LANES, (half + 1) * LANES)
        weights_ref[:, lanes] = tall_ref[pl.ds(half, slots, stride=2), :]
        for part in range(2):
            vec_ref[part:part + 1, lanes] = packed_ref[part * 2 + half:part * 2 + half + 1, :]


def power_call(part, vwin, idx, bins, deg, count):
    groups = idx.shape[0] // 8
    vmem = pl.BlockSpec(memory_space=pltpu.VMEM)
    n = len(STEPS)
    dma = pltpu.SemaphoreType.DMA
    return pl.pallas_call(
        lambda *refs: power_kernel(count, groups, *refs),
        out_shape=(jax.ShapeDtypeStruct(idx.shape, jnp.float32), jax.ShapeDtypeStruct((8, LANES), jnp.float32)),
        in_specs=[vmem] * 5,
        out_specs=(vmem, vmem),
        scratch_shapes=[pltpu.VMEM((groups, 8, LANES), jnp.float32)] * 5 + [pltpu.VMEM((7, PIECE, LANES), jnp.float32), pltpu.VMEM((8, PIECE, LANES), jnp.float32),
                        pltpu.VMEM((BLOCKS, 8, LANES), jnp.float32), pltpu.VMEM((BLOCKS, 8, LANES), jnp.float32),
                        pltpu.VMEM((8, 8, LANES), jnp.float32), pltpu.VMEM((8, 8, LANES), jnp.float32),
                        dma((7,)), dma((7,)), dma((7,)), dma((7,)), dma((2, n)), dma((2, n)), dma((2, 7)), dma((2, 7))],
        compiler_params=pltpu.CompilerParams(collective_id=1, has_side_effects=True),
        name="power",
    )(part, vwin, idx, bins, deg)


def shards(coef, neighbours, rot_bin, degree, v_init):
    count = lax.axis_size("img")
    window, vwin, idx, bins = window_call(coef, neighbours, rot_bin, v_init, count)
    groups = lambda value: value.reshape(TALL // 8, 8, LANES)
    part = pair_call(groups(idx), window, groups(bins))
    tall, packed = power_call(part.reshape(8, PIECE, LANES), vwin, idx, bins, degree.reshape(2, LANES), count)
    vmem = pl.BlockSpec(memory_space=pltpu.VMEM)
    weights, vector = pl.pallas_call(
        finish_kernel,
        out_shape=(jax.ShapeDtypeStruct(neighbours.shape, jnp.float32), jax.ShapeDtypeStruct(v_init.shape, jnp.float32)),
        in_specs=[vmem] * 2,
        out_specs=(vmem, vmem),
        name="finish",
    )(tall, packed)
    return vector, weights


def solution(mesh):
    return jax.shard_map(
        shards,
        mesh=mesh,
        in_specs=(P("img", "freq"), P(None, "img"), P(None, "img"), P("img"), P(None, "img")),
        out_specs=(P(None, "img"), P(None, "img")),
        check_vma=False,
    )
```

```python
import math

import jax
import jax.numpy as jnp
from jax import lax
from jax.experimental import pallas as pl
from jax.experimental.pallas import tpu as pltpu
from jax.sharding import PartitionSpec as P

RADIAL = 8
BINS = 360
ITERS = 3
LANES = 128
SPAN = 8
BLOCKS = 2 * SPAN + 1
TALL = 104

sharpness = 64.0
norm_eps = 1e-05
mean_eps = 1e-06

MESH = pl.DeviceIdType.MESH
STEPS = [sign * dist for dist in range(SPAN, 0, -1) for sign in (1, -1)]


def cos_sin_turns(units):
    turns = jnp.floor((units + 0.5) * (1.0 / BINS))
    rest = units - turns * BINS
    quarter = jnp.floor((rest + 45.0) * (1.0 / 90.0) + 1e-3)
    x = (rest - quarter * 90.0) * (math.pi / 180.0)
    y = x * x
    s = x * (1.0 + y * (-1.0 / 6 + y * (1.0 / 120 + y * (-1.0 / 5040 + y * (1.0 / 362880)))))
    c = 1.0 + y * (-0.5 + y * (1.0 / 24 + y * (-1.0 / 720 + y * (1.0 / 40320))))
    odd = (quarter == 1.0) | (quarter == 3.0)
    cos = jnp.where(odd, s, c)
    sin = jnp.where(odd, c, s)
    cos = jnp.where((quarter == 1.0) | (quarter == 2.0), -cos, cos)
    sin = jnp.where((quarter == 2.0) | (quarter == 3.0), -sin, sin)
    return cos, sin


def img_at(me, step, count):
    return {"img": lax.rem(me + (step + count), count)}


def greet(targets):
    barrier = pltpu.get_barrier_semaphore()
    for target in targets:
        pl.semaphore_signal(barrier, inc=1, device_id=target, device_id_type=MESH)
    return lambda: pl.semaphore_wait(barrier, len(targets))


def ring(me, mine_z, mine_y):
    y_at = lambda q: {"img": mine_z * 8 + lax.rem(mine_y + q, 8)}
    z_at = lambda q: {"img": lax.rem(mine_z + q, 8) * 8 + mine_y}
    return y_at, z_at


def landing_slot(mine_y, hop):
    if hop == -SPAN:
        return 2 * SPAN
    row = lax.div(mine_y + (hop + SPAN), SPAN) - 1
    return mine_y + SPAN * row * row


def window_part(count, met, coef_ref, nei_ref, bin_ref, v_ref, win_ref, vwin_ref, idx_ref, bins_ref, message, squares,
                y_send, y_recv, z_send, z_recv, v_send, v_recv, s_send, s_recv, local):
    me = lax.axis_index("img")
    mine = lax.axis_index("freq")
    y, z = lax.rem(me, 8), lax.div(me, 8)
    y_at, z_at = ring(me, z, y)
    freq_at = lambda q: {"freq": lax.rem(mine + q, 8)}
    own = pltpu.make_async_copy(coef_ref, win_ref.at[y], local.at[0])
    own.start()
    ones = jnp.ones((8, 2 * LANES), jnp.bfloat16)
    for half in range(2):
        piece = coef_ref[half * LANES:(half + 1) * LANES, :].astype(jnp.float32)
        sums = lane_sums(ones, split_exact(piece * piece))
        if half == 0:
            first_sums = sums
    sub = lax.broadcasted_iota(jnp.int32, (8, LANES), 0)
    squares[mine] = jnp.where(sub % 2 == 0, first_sums, sums)
    met()

    def send(src, dst, ss, rs, target):
        copy = pltpu.make_async_remote_copy(
            src_ref=src, dst_ref=dst, send_sem=ss, recv_sem=rs, device_id=target, device_id_type=MESH)
        copy.start()
        return copy

    ways = (1, 7)
    chunk = lambda c: pl.ds(c * LANES, LANES)
    flows, rows = {}, []
    for c in range(2):
        for w in range(2):
            flows[w, 0, c] = send(coef_ref.at[chunk(c)], win_ref.at[y, chunk(c)], y_send.at[w, 0, c],
                                  y_recv.at[w, 0, c], y_at(ways[w]))
    for c in range(2):
        rows.append(send(coef_ref.at[chunk(c)], win_ref.at[8 + y, chunk(c)], z_send.at[7, c], z_recv.at[7, c], z_at(1)))
        rows.append(send(coef_ref.at[chunk(c)], win_ref.at[16, chunk(c)], z_send.at[8, c], z_recv.at[8, c], z_at(7)))
    sums = [send(squares.at[mine], squares.at[mine], s_send.at[q - 1], s_recv.at[q - 1], freq_at(q))
            for q in range(1, 8)]

    slots = nei_ref.shape[0]
    nei = nei_ref[...]
    block = nei >> 8
    hop = ((block - me + (SPAN + count)) & (count - 1)) - SPAN
    slot = jnp.where(hop == SPAN, 2 * SPAN, (block & 7) + jnp.where((block >> 3) != z, SPAN, 0))
    place = slot * (2 * LANES) + (nei & (2 * LANES - 1))
    for half in range(2):
        idx_ref[pl.ds(half, slots, stride=2), :] = place[:, half * LANES:(half + 1) * LANES]
        bins_ref[pl.ds(half, slots, stride=2), :] = bin_ref[:, half * LANES:(half + 1) * LANES]
    idx_ref[2 * slots:, :] = jnp.zeros((TALL - 2 * slots, LANES), jnp.int32)
    bins_ref[2 * slots:, :] = jnp.zeros((TALL - 2 * slots, LANES), jnp.int32)

    small = []
    for q in range(1, 5):
        for c in range(2):
            for w in range(2):
                if q == 4 and w != c:
                    continue
                block_at = lax.rem(y + (8 - q if w == 0 else q), 8)
                turn = lax.div(y - q + 8, 8) if w == 0 else lax.div(y + q, 8)
                if q == 4:
                    turn = lax.div(y + 4, 8)
                flows[w, q - 1, c].wait_recv()
                held = win_ref.at[block_at, chunk(c)]
                if q < 3 or (q == 3 and w == c):
                    flows[w, q, c] = send(held, held, y_send.at[w, q, c], y_recv.at[w, q, c], y_at(ways[w]))
                at = (q - 1) * 2 + w if q < 4 else 6
                rows.append(send(held, win_ref.at[8 + block_at, chunk(c)], z_send.at[at, c], z_recv.at[at, c],
                                 z_at(1 + 6 * turn)))
        if q == 1:
            for copy in sums:
                copy.wait()
            total = squares[0]
            for other in range(1, 8):
                total = total + squares[other]
            packed = total
            for part in range(2):
                for half in range(2):
                    value = v_ref[part:part + 1, half * LANES:(half + 1) * LANES]
                    packed = jnp.where(sub == part * 2 + half, value, packed)
            message[...] = packed
            vwin_ref[y] = packed
            small = [send(message, vwin_ref.at[landing_slot(y, step)], v_send.at[n], v_recv.at[n],
                          img_at(me, step, count)) for n, step in enumerate(STEPS)]
    for copy in small + rows:
        copy.wait()
    for copy in flows.values():
        copy.wait_send()
    own.wait()


def split_exact(value):
    high = value.astype(jnp.bfloat16)
    low = (value - high.astype(jnp.float32)).astype(jnp.bfloat16)
    return jnp.concatenate([high, low], axis=1)


def lane_sums(select, value):
    return lax.dot_general(select, value, (((1,), (1,)), ((), ())), preferred_element_type=jnp.float32)


def pair_part(groups, idx_ref, win_ref, vwin_ref, bins_ref, out_ref, cos_buf, sin_buf, real_buf, imag_buf, root_buf,
              wide, own_tile, turned, places, arrived, tiles):
    rows = win_ref.shape[1]
    eight = lambda group: pl.ds(group * 8 if isinstance(group, int) else pl.multiple_of(group * 8, 8), 8)
    fetch = lambda group, at: pltpu.make_async_copy(idx_ref.at[eight(group)], places[at], arrived.at[at])
    fetch(0, 0).start()
    fetch(1, 1).start()
    first = lax.axis_index("freq") * (LANES // (2 * RADIAL))
    lane = lax.broadcasted_iota(jnp.int32, (8, 2 * LANES), 1)
    sub = lax.broadcasted_iota(jnp.int32, (8, 2 * LANES), 0)
    select = jnp.where((lane % LANES) // (2 * RADIAL) == sub, 1.0, 0.0).astype(jnp.bfloat16)
    freq = (first + lax.broadcasted_iota(jnp.int32, (8, LANES), 0)).astype(jnp.float32)
    line = lax.broadcasted_iota(jnp.int32, (8, LANES), 0)

    for block in range(BLOCKS):
        wide[block * rows:(block + 1) * rows, :] = win_ref[block].astype(jnp.float32)
    here = lax.rem(lax.axis_index("img"), 8)
    own = win_ref[here].astype(jnp.float32)
    own_sq = vwin_ref[here]
    own_root = lax.rsqrt(jnp.where(line % 2 == 0, own_sq[4:5], own_sq[5:6]) + norm_eps)
    own_tile[...] = own
    column = lax.broadcasted_iota(jnp.int32, own.shape, 1)
    turned[...] = jnp.where(column % (2 * RADIAL) < RADIAL,
                            pltpu.roll(own, LANES - RADIAL, 1), -pltpu.roll(own, RADIAL, 1))
    for group in range(groups, 16):
        out_ref[group] = jnp.zeros((8, LANES), jnp.float32)

    def one_group(group, at, then=None):
        fetch(group, at).wait()
        place = places[at]
        for n in range(8):
            for pair in range(LANES):
                tiles[n][pair:pair + 1, :] = wide[pl.ds(place[n, pair], 1), :]
        if then is not None:
            fetch(then, at).start()
        result = jnp.zeros((8, LANES), jnp.float32)
        spots = idx_ref[eight(group), :]
        spins = bins_ref[eight(group), :].astype(jnp.float32)
        ((real, imag, square),) = pick([spots & (LANES - 1)], [spots >> 7], vwin_ref, (0, 2, 4))
        cos, sin = cos_sin_turns(spins)
        cos_buf[group] = cos
        sin_buf[group] = sin
        real_buf[group] = cos * real - sin * imag
        imag_buf[group] = sin * real + cos * imag
        root_buf[group] = lax.rsqrt(square + norm_eps) * own_root
        for n in range(8):
            half = slice((n % 2) * LANES, (n % 2 + 1) * LANES)
            other = tiles[n][...]
            real = split_exact(own_tile[half, :] * other)
            imag = split_exact(turned[half, :] * other)
            sums = lane_sums(select, jnp.concatenate([real, imag], axis=0))
            units = spins[n:n + 1, :] * freq
            cos, sin = cos_sin_turns(units)
            terms = sums[:, :LANES] * cos - sums[:, LANES:] * sin
            result = jnp.where(line == n, jnp.sum(terms, axis=0, keepdims=True), result)
        out_ref[group] = result

    def body(step, carry):
        one_group(2 * step, 0, 2 * step + 2)
        one_group(2 * step + 1, 1, jnp.minimum(2 * step + 3, groups - 1))
        return carry

    lax.fori_loop(0, groups // 2, body, 0)
    one_group(groups - 1, 0)
    fetch(groups - 1, 1).wait()


def pick(low, high, ref, lines):
    found = []
    for where, at in zip(low, high):
        got = [None] * len(lines)
        for row in range(BLOCKS * 2):
            hit = at == row
            for n, line in enumerate(lines):
                first = line + row % 2
                wide = jnp.broadcast_to(ref[row // 2, first:first + 1, :], (8, LANES))
                new = jnp.take_along_axis(wide, where, axis=1, mode="promise_in_bounds")
                got[n] = new if row == 0 else jnp.where(hit, new, got[n])
        found.append(got)
    return found


def fold(total):
    total = total + pltpu.roll(total, 4, 0)
    return total + pltpu.roll(total, 2, 0)


def power_part(count, groups, part_ref, idx_ref, deg_ref, weights_ref, vec_ref,
               cos_buf, sin_buf, real_buf, imag_buf, root_buf, rs_buf, ag_buf, vec1, vec2, ynorm, znorm,
               rs_send, rs_recv, ag_send, ag_recv, v_send, v_recv, n_send, n_recv):
    me = lax.axis_index("img")
    mine = lax.axis_index("freq")
    y, z = lax.rem(me, 8), lax.div(me, 8)
    freq_at = lambda q: {"freq": lax.rem(mine + q, 8)}
    y_at, z_at = ring(me, z, y)
    two = lambda piece: pl.ds(2 * piece, 2)
    copies = []
    for q in range(1, 8):
        copy = pltpu.make_async_remote_copy(
            src_ref=part_ref.at[two(lax.rem(mine + q, 8))], dst_ref=rs_buf.at[q - 1],
            send_sem=rs_send.at[q - 1], recv_sem=rs_recv.at[q - 1], device_id=freq_at(q), device_id_type=MESH)
        copy.start()
        copies.append(copy)
    for copy in copies:
        copy.wait()
    total = part_ref[two(mine)]
    for q in range(7):
        total = total + rs_buf[q]
    ag_buf[two(mine)] = total
    copies = []
    for q in range(1, 8):
        copy = pltpu.make_async_remote_copy(
            src_ref=ag_buf.at[two(mine)], dst_ref=ag_buf.at[two(mine)],
            send_sem=ag_send.at[q - 1], recv_sem=ag_recv.at[q - 1], device_id=freq_at(q), device_id_type=MESH)
        copy.start()
        copies.append(copy)
    for copy in copies:
        copy.wait()

    sub = lax.broadcasted_iota(jnp.int32, (8, LANES), 0)
    degree = jnp.where(sub % 2 == 0, deg_ref[0:1, :], deg_ref[1:2, :])
    low = [idx_ref[m * 8:(m + 1) * 8, :] & (LANES - 1) for m in range(groups)]
    high = [idx_ref[m * 8:(m + 1) * 8, :] >> 7 for m in range(groups)]
    denom = jnp.zeros((8, LANES), jnp.float32)
    for m in range(groups):
        cos_sim = ag_buf[m] * root_buf[m]
        raw = jnp.where((sub // 2 + m * 4) < degree, jnp.exp(sharpness * cos_sim), 0.0)
        weights_ref[m * 8:(m + 1) * 8, :] = raw
        denom = denom + raw
    share = 1.0 / fold(denom)
    for m in range(groups):
        weights_ref[m * 8:(m + 1) * 8, :] = weights_ref[m * 8:(m + 1) * 8, :] * share

    norms = []
    source = None
    for step in range(ITERS):
        real = imag = jnp.zeros((8, LANES), jnp.float32)
        picked = pick(low, high, source, (0, 2)) if step else [None] * groups
        for m, at in enumerate(picked):
            weight = weights_ref[m * 8:(m + 1) * 8, :]
            if step:
                real_at, imag_at = at
                real = real + weight * (cos_buf[m] * real_at - sin_buf[m] * imag_at)
                imag = imag + weight * (sin_buf[m] * real_at + cos_buf[m] * imag_at)
            else:
                real = real + weight * real_buf[m]
                imag = imag + weight * imag_buf[m]
        real, imag = fold(real), fold(imag)
        square = real * real + imag * imag
        norms.append(square + pltpu.roll(square, 1, 0))
        packed = jnp.where(sub % 4 < 2, real, imag)
        if step < ITERS - 1:
            into = (vec1, vec2)[step]
            into[y] = packed
            copies = []
            for n, hop in enumerate(STEPS):
                copy = pltpu.make_async_remote_copy(
                    src_ref=into.at[y], dst_ref=into.at[landing_slot(y, hop)], send_sem=v_send.at[step, n],
                    recv_sem=v_recv.at[step, n], device_id=img_at(me, hop, count), device_id_type=MESH)
                copy.start()
                copies.append(copy)
            for copy in copies:
                copy.wait()
            source = into

    message = jnp.where(sub == 0, norms[0], jnp.where(sub == 1, norms[1], norms[2]))
    for axis, (buf, where) in enumerate(((ynorm, y_at), (znorm, z_at))):
        buf[7] = message
        copies = []
        for q in range(1, 8):
            copy = pltpu.make_async_remote_copy(
                src_ref=buf.at[7], dst_ref=buf.at[q - 1], send_sem=n_send.at[axis, q - 1],
                recv_sem=n_recv.at[axis, q - 1], device_id=where(q), device_id_type=MESH)
            copy.start()
            copies.append(copy)
        for copy in copies:
            copy.wait()
        for q in range(7):
            message = message + buf[q]
    sums = jnp.sum(message, axis=1, keepdims=True)
    images = count * 2 * LANES
    scale = lax.rsqrt(sums[0:1] / images + mean_eps)
    for step in range(1, ITERS):
        scale = scale * lax.rsqrt(scale * scale * sums[step:step + 1] / images + mean_eps)
    vec_ref[...] = packed * scale


def finish_kernel(tall_ref, packed_ref, weights_ref, vec_ref):
    slots = weights_ref.shape[0]
    for half in range(2):
        lanes = slice(half * LANES, (half + 1) * LANES)
        weights_ref[:, lanes] = tall_ref[pl.ds(half, slots, stride=2), :]
        for part in range(2):
            vec_ref[part:part + 1, lanes] = packed_ref[part * 2 + half:part * 2 + half + 1, :]


def whole_call(coef, neighbours, rot_bin, deg, v_init, count):
    rows, width = coef.shape
    groups = TALL // 8
    n = len(STEPS)
    vmem = pl.BlockSpec(memory_space=pltpu.VMEM)
    dma = pltpu.SemaphoreType.DMA
    real = lambda *shape: pltpu.VMEM(shape, jnp.float32)
    window = [pltpu.VMEM((BLOCKS, rows, width), coef.dtype), real(BLOCKS, 8, LANES),
              pltpu.VMEM((TALL, LANES), jnp.int32), pltpu.VMEM((TALL, LANES), jnp.int32),
              real(8, LANES), real(8, 8, LANES), dma((2, 4, 2)), dma((2, 4, 2)), dma((9, 2)), dma((9, 2)),
              dma((n,)), dma((n,)), dma((7,)), dma((7,)), dma((1,))]
    shared = [real(16, 8, LANES)] + [real(groups, 8, LANES)] * 5
    pairs = [real(BLOCKS * rows, width), real(rows, width), real(rows, width), pltpu.SMEM((8, LANES), jnp.int32),
             pltpu.SMEM((8, LANES), jnp.int32), dma((2,))] + [real(LANES, LANES)] * 8
    power = [real(7, 2, 8, LANES), real(16, 8, LANES), real(BLOCKS, 8, LANES), real(BLOCKS, 8, LANES),
             real(8, 8, LANES), real(8, 8, LANES),
             dma((7,)), dma((7,)), dma((7,)), dma((7,)), dma((2, n)), dma((2, n)), dma((2, 7)), dma((2, 7))]

    def kernel(coef_ref, nei_ref, bin_ref, deg_ref, v_ref, weights_ref, vec_ref, *scratch):
        me = lax.axis_index("img")
        mine = lax.axis_index("freq")
        y_at, z_at = ring(me, lax.div(me, 8), lax.rem(me, 8))
        met = greet([img_at(me, step, count) for step in STEPS] + [{"freq": lax.rem(mine + q, 8)} for q in range(1, 8)]
                    + [y_at(q) for q in range(1, 8)] + [z_at(q) for q in range(1, 8)])
        cut = [0]
        for part in (window, shared, pairs, power):
            cut.append(cut[-1] + len(part))
        win, both, pair, last = [scratch[a:b] for a, b in zip(cut, cut[1:])]
        window_part(count, met, coef_ref, nei_ref, bin_ref, v_ref, *win)
        pair_part(groups, win[2], win[0], win[1], win[3], *both, *pair[:3], pair[3:5], pair[5], pair[6:])
        power_part(count, groups, both[0], win[2], deg_ref, weights_ref, vec_ref, *both[1:], *last)

    return pl.pallas_call(
        kernel,
        out_shape=(jax.ShapeDtypeStruct((TALL, LANES), jnp.float32), jax.ShapeDtypeStruct((8, LANES), jnp.float32)),
        in_specs=[vmem] * 5,
        out_specs=(vmem, vmem),
        scratch_shapes=window + shared + pairs + power,
        compiler_params=pltpu.CompilerParams(collective_id=0, has_side_effects=True),
        name="whole",
    )(coef, neighbours, rot_bin, deg, v_init)


def shards(coef, neighbours, rot_bin, degree, v_init):
    count = lax.axis_size("img")
    tall, packed = whole_call(coef, neighbours, rot_bin, degree.reshape(2, LANES), v_init, count)
    vmem = pl.BlockSpec(memory_space=pltpu.VMEM)
    weights, vector = pl.pallas_call(
        finish_kernel,
        out_shape=(jax.ShapeDtypeStruct(neighbours.shape, jnp.float32), jax.ShapeDtypeStruct(v_init.shape, jnp.float32)),
        in_specs=[vmem] * 2,
        out_specs=(vmem, vmem),
        name="finish",
    )(tall, packed)
    return vector, weights


def solution(mesh):
    return jax.shard_map(
        shards,
        mesh=mesh,
        in_specs=(P("img", "freq"), P(None, "img"), P(None, "img"), P("img"), P(None, "img")),
        out_specs=(P(None, "img"), P(None, "img")),
        check_vma=False,
    )
```

```python
import math

import jax
import jax.numpy as jnp
from jax import lax
from jax.experimental import pallas as pl
from jax.experimental.pallas import tpu as pltpu
from jax.sharding import PartitionSpec as P

RADIAL = 8
BINS = 360
ITERS = 3
LANES = 128
SPAN = 8
BLOCKS = 2 * SPAN + 1
TALL = 104

sharpness = 64.0
norm_eps = 1e-05
mean_eps = 1e-06

MESH = pl.DeviceIdType.MESH
STEPS = [sign * dist for dist in range(SPAN, 0, -1) for sign in (1, -1)]


def cos_sin_turns(units):
    turns = jnp.floor((units + 0.5) * (1.0 / BINS))
    rest = units - turns * BINS
    quarter = jnp.floor((rest + 45.0) * (1.0 / 90.0) + 1e-3)
    x = (rest - quarter * 90.0) * (math.pi / 180.0)
    y = x * x
    s = x * (1.0 + y * (-1.0 / 6 + y * (1.0 / 120 + y * (-1.0 / 5040 + y * (1.0 / 362880)))))
    c = 1.0 + y * (-0.5 + y * (1.0 / 24 + y * (-1.0 / 720 + y * (1.0 / 40320))))
    odd = (quarter == 1.0) | (quarter == 3.0)
    cos = jnp.where(odd, s, c)
    sin = jnp.where(odd, c, s)
    cos = jnp.where((quarter == 1.0) | (quarter == 2.0), -cos, cos)
    sin = jnp.where((quarter == 2.0) | (quarter == 3.0), -sin, sin)
    return cos, sin


def img_at(me, step, count):
    return {"img": lax.rem(me + (step + count), count)}


def greet(targets):
    barrier = pltpu.get_barrier_semaphore()
    for target in targets:
        pl.semaphore_signal(barrier, inc=1, device_id=target, device_id_type=MESH)
    return lambda: pl.semaphore_wait(barrier, len(targets))


def ring(me, mine_z, mine_y):
    y_at = lambda q: {"img": mine_z * 8 + lax.rem(mine_y + q, 8)}
    z_at = lambda q: {"img": lax.rem(mine_z + q, 8) * 8 + mine_y}
    return y_at, z_at


def landing_slot(mine_y, hop):
    if hop == -SPAN:
        return 2 * SPAN
    row = lax.div(mine_y + (hop + SPAN), SPAN) - 1
    return mine_y + SPAN * row * row


def window_part(count, met, coef_ref, nei_ref, bin_ref, v_ref, wide, win_ref, vwin_ref, idx_ref, bins_ref, message,
                squares,                y_send, y_recv, z_send, z_recv, v_send, v_recv, s_send, s_recv):
    me = lax.axis_index("img")
    mine = lax.axis_index("freq")
    y, z = lax.rem(me, 8), lax.div(me, 8)
    y_at, z_at = ring(me, z, y)
    freq_at = lambda q: {"freq": lax.rem(mine + q, 8)}
    images = coef_ref.shape[0]

    def widen(slot, value):
        start = slot * images if isinstance(slot, int) else pl.multiple_of(slot * images, images)
        wide[pl.ds(start, images), :] = value.astype(jnp.float32)

    widen(y, coef_ref[...])
    ones = jnp.ones((8, 2 * LANES), jnp.bfloat16)
    for half in range(2):
        piece = coef_ref[half * LANES:(half + 1) * LANES, :].astype(jnp.float32)
        sums = lane_sums(ones, split_exact(piece * piece))
        if half == 0:
            first_sums = sums
    sub = lax.broadcasted_iota(jnp.int32, (8, LANES), 0)
    squares[mine] = jnp.where(sub % 2 == 0, first_sums, sums)
    met()

    def send(src, dst, ss, rs, target):
        copy = pltpu.make_async_remote_copy(
            src_ref=src, dst_ref=dst, send_sem=ss, recv_sem=rs, device_id=target, device_id_type=MESH)
        copy.start()
        return copy

    ways = (1, 7)
    chunk = lambda c: pl.ds(c * LANES, LANES)
    flows, rows, landed = {}, [], {7: 8 + y, 8: 16}
    across = {at: [] for at in range(9)}
    for c in range(2):
        for w in range(2):
            flows[w, 0, c] = send(coef_ref.at[chunk(c)], win_ref.at[y, chunk(c)], y_send.at[w, 0, c],
                                  y_recv.at[w, 0, c], y_at(ways[w]))
    for c in range(2):
        across[7].append(send(coef_ref.at[chunk(c)], win_ref.at[8 + y, chunk(c)], z_send.at[7, c], z_recv.at[7, c],
                              z_at(1)))
        across[8].append(send(coef_ref.at[chunk(c)], win_ref.at[16, chunk(c)], z_send.at[8, c], z_recv.at[8, c],
                              z_at(7)))
    sums = [send(squares.at[mine], squares.at[mine], s_send.at[q - 1], s_recv.at[q - 1], freq_at(q))
            for q in range(1, 8)]

    slots = nei_ref.shape[0]
    nei = nei_ref[...]
    block = nei >> 8
    hop = ((block - me + (SPAN + count)) & (count - 1)) - SPAN
    slot = jnp.where(hop == SPAN, 2 * SPAN, (block & 7) + jnp.where((block >> 3) != z, SPAN, 0))
    place = slot * (2 * LANES) + (nei & (2 * LANES - 1))
    for half in range(2):
        idx_ref[pl.ds(half, slots, stride=2), :] = place[:, half * LANES:(half + 1) * LANES]
        bins_ref[pl.ds(half, slots, stride=2), :] = bin_ref[:, half * LANES:(half + 1) * LANES]
    idx_ref[2 * slots:, :] = jnp.zeros((TALL - 2 * slots, LANES), jnp.int32)
    bins_ref[2 * slots:, :] = jnp.zeros((TALL - 2 * slots, LANES), jnp.int32)

    small = []
    for q in range(1, 5):
        for c in range(2):
            for w in range(2):
                if q == 4 and w != c:
                    continue
                block_at = lax.rem(y + (8 - q if w == 0 else q), 8)
                turn = lax.div(y - q + 8, 8) if w == 0 else lax.div(y + q, 8)
                if q == 4:
                    turn = lax.div(y + 4, 8)
                flows[w, q - 1, c].wait_recv()
                held = win_ref.at[block_at, chunk(c)]
                if q < 3 or (q == 3 and w == c):
                    flows[w, q, c] = send(held, held, y_send.at[w, q, c], y_recv.at[w, q, c], y_at(ways[w]))
                at = (q - 1) * 2 + w if q < 4 else 6
                across[at].append(send(held, win_ref.at[8 + block_at, chunk(c)], z_send.at[at, c], z_recv.at[at, c],
                                       z_at(1 + 6 * turn)))
                landed[at] = 8 + block_at
                if c == 1:
                    rows.append(block_at)
        while rows:
            slot = rows.pop()
            widen(slot, win_ref[slot])
        if q == 1:
            for copy in sums:
                copy.wait()
            total = squares[0]
            for other in range(1, 8):
                total = total + squares[other]
            packed = total
            for part in range(2):
                for half in range(2):
                    value = v_ref[part:part + 1, half * LANES:(half + 1) * LANES]
                    packed = jnp.where(sub == part * 2 + half, value, packed)
            message[...] = packed
            vwin_ref[y] = packed
            small = [send(message, vwin_ref.at[landing_slot(y, step)], v_send.at[n], v_recv.at[n],
                          img_at(me, step, count)) for n, step in enumerate(STEPS)]
    for at in (7, 8, 0, 1, 2, 3, 4, 5, 6):
        for copy in across[at]:
            copy.wait()
        widen(landed[at], win_ref[landed[at]])
    for copy in small:
        copy.wait()
    for copy in flows.values():
        copy.wait_send()


def split_exact(value):
    high = value.astype(jnp.bfloat16)
    low = (value - high.astype(jnp.float32)).astype(jnp.bfloat16)
    return jnp.concatenate([high, low], axis=1)


def lane_sums(select, value):
    return lax.dot_general(select, value, (((1,), (1,)), ((), ())), preferred_element_type=jnp.float32)


def pair_part(groups, idx_ref, coef_ref, vwin_ref, bins_ref, out_ref, cos_buf, sin_buf, real_buf, imag_buf, root_buf,
              wide, own_tile, turned, places, arrived, tiles):
    eight = lambda group: pl.ds(group * 8 if isinstance(group, int) else pl.multiple_of(group * 8, 8), 8)
    fetch = lambda group, at: pltpu.make_async_copy(idx_ref.at[eight(group)], places[at], arrived.at[at])
    fetch(0, 0).start()
    fetch(1, 1).start()
    first = lax.axis_index("freq") * (LANES // (2 * RADIAL))
    lane = lax.broadcasted_iota(jnp.int32, (8, 2 * LANES), 1)
    sub = lax.broadcasted_iota(jnp.int32, (8, 2 * LANES), 0)
    select = jnp.where((lane % LANES) // (2 * RADIAL) == sub, 1.0, 0.0).astype(jnp.bfloat16)
    freq = (first + lax.broadcasted_iota(jnp.int32, (8, LANES), 0)).astype(jnp.float32)
    line = lax.broadcasted_iota(jnp.int32, (8, LANES), 0)

    here = lax.rem(lax.axis_index("img"), 8)
    own = coef_ref[...].astype(jnp.float32)
    own_sq = vwin_ref[here]
    own_root = lax.rsqrt(jnp.where(line % 2 == 0, own_sq[4:5], own_sq[5:6]) + norm_eps)
    own_tile[...] = own
    column = lax.broadcasted_iota(jnp.int32, own.shape, 1)
    turned[...] = jnp.where(column % (2 * RADIAL) < RADIAL,
                            pltpu.roll(own, LANES - RADIAL, 1), -pltpu.roll(own, RADIAL, 1))
    for group in range(groups, 16):
        out_ref[group] = jnp.zeros((8, LANES), jnp.float32)

    def one_group(group, at, then=None):
        fetch(group, at).wait()
        place = places[at]
        spots = idx_ref[eight(group), :]
        spins = bins_ref[eight(group), :].astype(jnp.float32)
        result = jnp.zeros((8, LANES), jnp.float32)
        for n in range(9):
            if n < 8:
                for pair in range(LANES):
                    tiles[n][pair:pair + 1, :] = wide[pl.ds(place[n, pair], 1), :]
            if n == 0:
                ((real, imag, square),) = pick([spots & (LANES - 1)], [spots >> 7], vwin_ref, (0, 2, 4))
                cos, sin = cos_sin_turns(spins)
                cos_buf[group] = cos
                sin_buf[group] = sin
                real_buf[group] = cos * real - sin * imag
                imag_buf[group] = sin * real + cos * imag
                root_buf[group] = lax.rsqrt(square + norm_eps) * own_root
                continue
            done = n - 1
            half = slice((done % 2) * LANES, (done % 2 + 1) * LANES)
            other = tiles[done][...]
            real = split_exact(own_tile[half, :] * other)
            imag = split_exact(turned[half, :] * other)
            sums = lane_sums(select, jnp.concatenate([real, imag], axis=0))
            cos, sin = cos_sin_turns(spins[done:done + 1, :] * freq)
            terms = sums[:, :LANES] * cos - sums[:, LANES:] * sin
            result = jnp.where(line == done, jnp.sum(terms, axis=0, keepdims=True), result)
        out_ref[group] = result
        if then is not None:
            fetch(then, at).start()

    def body(step, carry):
        one_group(2 * step, 0, 2 * step + 2)
        one_group(2 * step + 1, 1, jnp.minimum(2 * step + 3, groups - 1))
        return carry

    lax.fori_loop(0, groups // 2, body, 0)
    one_group(groups - 1, 0)
    fetch(groups - 1, 1).wait()


def pick(low, high, ref, lines):
    found = []
    for where, at in zip(low, high):
        got = [None] * len(lines)
        for row in range(BLOCKS * 2):
            hit = at == row
            for n, line in enumerate(lines):
                first = line + row % 2
                wide = jnp.broadcast_to(ref[row // 2, first:first + 1, :], (8, LANES))
                new = jnp.take_along_axis(wide, where, axis=1, mode="promise_in_bounds")
                got[n] = new if row == 0 else jnp.where(hit, new, got[n])
        found.append(got)
    return found


def fold(total):
    total = total + pltpu.roll(total, 4, 0)
    return total + pltpu.roll(total, 2, 0)


def power_part(count, groups, part_ref, idx_ref, deg_ref, weights_ref, vec_ref,
               cos_buf, sin_buf, real_buf, imag_buf, root_buf, rs_buf, ag_buf, vec1, vec2, ynorm, znorm,
               rs_send, rs_recv, ag_send, ag_recv, v_send, v_recv, n_send, n_recv):
    me = lax.axis_index("img")
    mine = lax.axis_index("freq")
    y, z = lax.rem(me, 8), lax.div(me, 8)
    freq_at = lambda q: {"freq": lax.rem(mine + q, 8)}
    y_at, z_at = ring(me, z, y)
    two = lambda piece: pl.ds(2 * piece, 2)
    copies = []
    for q in range(1, 8):
        copy = pltpu.make_async_remote_copy(
            src_ref=part_ref.at[two(lax.rem(mine + q, 8))], dst_ref=rs_buf.at[q - 1],
            send_sem=rs_send.at[q - 1], recv_sem=rs_recv.at[q - 1], device_id=freq_at(q), device_id_type=MESH)
        copy.start()
        copies.append(copy)
    for copy in copies:
        copy.wait()
    total = part_ref[two(mine)]
    for q in range(7):
        total = total + rs_buf[q]
    ag_buf[two(mine)] = total
    copies = []
    for q in range(1, 8):
        copy = pltpu.make_async_remote_copy(
            src_ref=ag_buf.at[two(mine)], dst_ref=ag_buf.at[two(mine)],
            send_sem=ag_send.at[q - 1], recv_sem=ag_recv.at[q - 1], device_id=freq_at(q), device_id_type=MESH)
        copy.start()
        copies.append(copy)
    for copy in copies:
        copy.wait()

    sub = lax.broadcasted_iota(jnp.int32, (8, LANES), 0)
    degree = jnp.where(sub % 2 == 0, deg_ref[0:1, :], deg_ref[1:2, :])
    low = [idx_ref[m * 8:(m + 1) * 8, :] & (LANES - 1) for m in range(groups)]
    high = [idx_ref[m * 8:(m + 1) * 8, :] >> 7 for m in range(groups)]
    denom = jnp.zeros((8, LANES), jnp.float32)
    for m in range(groups):
        cos_sim = ag_buf[m] * root_buf[m]
        raw = jnp.where((sub // 2 + m * 4) < degree, jnp.exp(sharpness * cos_sim), 0.0)
        weights_ref[m * 8:(m + 1) * 8, :] = raw
        denom = denom + raw
    share = 1.0 / fold(denom)
    for m in range(groups):
        weights_ref[m * 8:(m + 1) * 8, :] = weights_ref[m * 8:(m + 1) * 8, :] * share

    norms = []
    source = None
    for step in range(ITERS):
        real = imag = jnp.zeros((8, LANES), jnp.float32)
        picked = pick(low, high, source, (0, 2)) if step else [None] * groups
        for m, at in enumerate(picked):
            weight = weights_ref[m * 8:(m + 1) * 8, :]
            if step:
                real_at, imag_at = at
                real = real + weight * (cos_buf[m] * real_at - sin_buf[m] * imag_at)
                imag = imag + weight * (sin_buf[m] * real_at + cos_buf[m] * imag_at)
            else:
                real = real + weight * real_buf[m]
                imag = imag + weight * imag_buf[m]
        real, imag = fold(real), fold(imag)
        square = real * real + imag * imag
        norms.append(square + pltpu.roll(square, 1, 0))
        packed = jnp.where(sub % 4 < 2, real, imag)
        if step < ITERS - 1:
            into = (vec1, vec2)[step]
            into[y] = packed
            copies = []
            for n, hop in enumerate(STEPS):
                copy = pltpu.make_async_remote_copy(
                    src_ref=into.at[y], dst_ref=into.at[landing_slot(y, hop)], send_sem=v_send.at[step, n],
                    recv_sem=v_recv.at[step, n], device_id=img_at(me, hop, count), device_id_type=MESH)
                copy.start()
                copies.append(copy)
            for copy in copies:
                copy.wait()
            source = into

    message = jnp.where(sub == 0, norms[0], jnp.where(sub == 1, norms[1], norms[2]))
    for axis, (buf, where) in enumerate(((ynorm, y_at), (znorm, z_at))):
        buf[7] = message
        copies = []
        for q in range(1, 8):
            copy = pltpu.make_async_remote_copy(
                src_ref=buf.at[7], dst_ref=buf.at[q - 1], send_sem=n_send.at[axis, q - 1],
                recv_sem=n_recv.at[axis, q - 1], device_id=where(q), device_id_type=MESH)
            copy.start()
            copies.append(copy)
        for copy in copies:
            copy.wait()
        for q in range(7):
            message = message + buf[q]
    sums = jnp.sum(message, axis=1, keepdims=True)
    images = count * 2 * LANES
    scale = lax.rsqrt(sums[0:1] / images + mean_eps)
    for step in range(1, ITERS):
        scale = scale * lax.rsqrt(scale * scale * sums[step:step + 1] / images + mean_eps)
    vec_ref[...] = packed * scale


def finish_kernel(tall_ref, packed_ref, weights_ref, vec_ref):
    slots = weights_ref.shape[0]
    for half in range(2):
        lanes = slice(half * LANES, (half + 1) * LANES)
        weights_ref[:, lanes] = tall_ref[pl.ds(half, slots, stride=2), :]
        for part in range(2):
            vec_ref[part:part + 1, lanes] = packed_ref[part * 2 + half:part * 2 + half + 1, :]


def whole_call(coef, neighbours, rot_bin, deg, v_init, count):
    rows, width = coef.shape
    groups = TALL // 8
    n = len(STEPS)
    vmem = pl.BlockSpec(memory_space=pltpu.VMEM)
    dma = pltpu.SemaphoreType.DMA
    real = lambda *shape: pltpu.VMEM(shape, jnp.float32)
    window = [pltpu.VMEM((BLOCKS, rows, width), coef.dtype), real(BLOCKS, 8, LANES),
              pltpu.VMEM((TALL, LANES), jnp.int32), pltpu.VMEM((TALL, LANES), jnp.int32),
              real(8, LANES), real(8, 8, LANES), dma((2, 4, 2)), dma((2, 4, 2)), dma((9, 2)), dma((9, 2)),
              dma((n,)), dma((n,)), dma((7,)), dma((7,))]
    shared = [real(16, 8, LANES)] + [real(groups, 8, LANES)] * 5
    pairs = [real(BLOCKS * rows, width), real(rows, width), real(rows, width), pltpu.SMEM((8, LANES), jnp.int32),
             pltpu.SMEM((8, LANES), jnp.int32), dma((2,))] + [real(LANES, LANES)] * 8
    power = [real(7, 2, 8, LANES), real(16, 8, LANES), real(BLOCKS, 8, LANES), real(BLOCKS, 8, LANES),
             real(8, 8, LANES), real(8, 8, LANES),
             dma((7,)), dma((7,)), dma((7,)), dma((7,)), dma((2, n)), dma((2, n)), dma((2, 7)), dma((2, 7))]

    def kernel(coef_ref, nei_ref, bin_ref, deg_ref, v_ref, weights_ref, vec_ref, *scratch):
        me = lax.axis_index("img")
        mine = lax.axis_index("freq")
        y_at, z_at = ring(me, lax.div(me, 8), lax.rem(me, 8))
        met = greet([img_at(me, step, count) for step in STEPS] + [{"freq": lax.rem(mine + q, 8)} for q in range(1, 8)]
                    + [y_at(q) for q in range(1, 8)] + [z_at(q) for q in range(1, 8)])
        cut = [0]
        for part in (window, shared, pairs, power):
            cut.append(cut[-1] + len(part))
        win, both, pair, last = [scratch[a:b] for a, b in zip(cut, cut[1:])]
        window_part(count, met, coef_ref, nei_ref, bin_ref, v_ref, pair[0], *win)
        pair_part(groups, win[2], coef_ref, win[1], win[3], *both, *pair[:3], pair[3:5], pair[5], pair[6:])
        power_part(count, groups, both[0], win[2], deg_ref, weights_ref, vec_ref, *both[1:], *last)

    return pl.pallas_call(
        kernel,
        out_shape=(jax.ShapeDtypeStruct((TALL, LANES), jnp.float32), jax.ShapeDtypeStruct((8, LANES), jnp.float32)),
        in_specs=[vmem] * 5,
        out_specs=(vmem, vmem),
        scratch_shapes=window + shared + pairs + power,
        compiler_params=pltpu.CompilerParams(collective_id=0, has_side_effects=True),
        name="whole",
    )(coef, neighbours, rot_bin, deg, v_init)


def shards(coef, neighbours, rot_bin, degree, v_init):
    count = lax.axis_size("img")
    tall, packed = whole_call(coef, neighbours, rot_bin, degree.reshape(2, LANES), v_init, count)
    vmem = pl.BlockSpec(memory_space=pltpu.VMEM)
    weights, vector = pl.pallas_call(
        finish_kernel,
        out_shape=(jax.ShapeDtypeStruct(neighbours.shape, jnp.float32), jax.ShapeDtypeStruct(v_init.shape, jnp.float32)),
        in_specs=[vmem] * 2,
        out_specs=(vmem, vmem),
        name="finish",
    )(tall, packed)
    return vector, weights


def solution(mesh):
    return jax.shard_map(
        shards,
        mesh=mesh,
        in_specs=(P("img", "freq"), P(None, "img"), P(None, "img"), P("img"), P(None, "img")),
        out_specs=(P(None, "img"), P(None, "img")),
        check_vma=False,
    )
```

```python
import math

import jax
import jax.numpy as jnp
from jax import lax
from jax.experimental import pallas as pl
from jax.experimental.pallas import tpu as pltpu
from jax.sharding import PartitionSpec as P

RADIAL = 8
BINS = 360
ITERS = 3
LANES = 128
SPAN = 8
BLOCKS = 2 * SPAN + 1
TALL = 104

sharpness = 64.0
norm_eps = 1e-05
mean_eps = 1e-06

MESH = pl.DeviceIdType.MESH
STEPS = [sign * dist for dist in range(SPAN, 0, -1) for sign in (1, -1)]


def cos_sin_turns(units):
    turns = jnp.floor((units + 0.5) * (1.0 / BINS))
    rest = units - turns * BINS
    quarter = jnp.floor((rest + 45.0) * (1.0 / 90.0) + 1e-3)
    x = (rest - quarter * 90.0) * (math.pi / 180.0)
    y = x * x
    s = x * (1.0 + y * (-1.0 / 6 + y * (1.0 / 120 + y * (-1.0 / 5040 + y * (1.0 / 362880)))))
    c = 1.0 + y * (-0.5 + y * (1.0 / 24 + y * (-1.0 / 720 + y * (1.0 / 40320))))
    odd = (quarter == 1.0) | (quarter == 3.0)
    cos = jnp.where(odd, s, c)
    sin = jnp.where(odd, c, s)
    cos = jnp.where((quarter == 1.0) | (quarter == 2.0), -cos, cos)
    sin = jnp.where((quarter == 2.0) | (quarter == 3.0), -sin, sin)
    return cos, sin


def img_at(me, step, count):
    return {"img": lax.rem(me + (step + count), count)}


def greet(targets):
    barrier = pltpu.get_barrier_semaphore()
    for target in targets:
        pl.semaphore_signal(barrier, inc=1, device_id=target, device_id_type=MESH)
    return lambda: pl.semaphore_wait(barrier, len(targets))


def ring(me, mine_z, mine_y):
    y_at = lambda q: {"img": mine_z * 8 + lax.rem(mine_y + q, 8)}
    z_at = lambda q: {"img": lax.rem(mine_z + q, 8) * 8 + mine_y}
    return y_at, z_at


def landing_slot(mine_y, hop):
    if hop == -SPAN:
        return 2 * SPAN
    row = lax.div(mine_y + (hop + SPAN), SPAN) - 1
    return mine_y + SPAN * row * row


def window_part(count, met, coef_ref, nei_ref, bin_ref, v_ref, win_ref, vwin_ref, idx_ref, bins_ref, message, squares,
                y_send, y_recv, z_send, z_recv, v_send, v_recv, s_send, s_recv, local):
    me = lax.axis_index("img")
    mine = lax.axis_index("freq")
    y, z = lax.rem(me, 8), lax.div(me, 8)
    y_at, z_at = ring(me, z, y)
    freq_at = lambda q: {"freq": lax.rem(mine + q, 8)}
    own = pltpu.make_async_copy(coef_ref, win_ref.at[y], local.at[0])
    own.start()
    ones = jnp.ones((8, 2 * LANES), jnp.bfloat16)
    for half in range(2):
        piece = coef_ref[half * LANES:(half + 1) * LANES, :].astype(jnp.float32)
        sums = lane_sums(ones, split_exact(piece * piece))
        if half == 0:
            first_sums = sums
    sub = lax.broadcasted_iota(jnp.int32, (8, LANES), 0)
    squares[mine] = jnp.where(sub % 2 == 0, first_sums, sums)
    met()

    def send(src, dst, ss, rs, target):
        copy = pltpu.make_async_remote_copy(
            src_ref=src, dst_ref=dst, send_sem=ss, recv_sem=rs, device_id=target, device_id_type=MESH)
        copy.start()
        return copy

    ways = (1, 7)
    quarter = coef_ref.shape[0] // 4
    chunk = lambda c: pl.ds(c * quarter, quarter)
    flows, rows = {}, []
    for c in range(4):
        for w in range(2):
            flows[w, 0, c] = send(coef_ref.at[chunk(c)], win_ref.at[y, chunk(c)], y_send.at[w, 0, c],
                                  y_recv.at[w, 0, c], y_at(ways[w]))
    for c in range(4):
        rows.append(send(coef_ref.at[chunk(c)], win_ref.at[8 + y, chunk(c)], z_send.at[7, c], z_recv.at[7, c], z_at(1)))
        rows.append(send(coef_ref.at[chunk(c)], win_ref.at[16, chunk(c)], z_send.at[8, c], z_recv.at[8, c], z_at(7)))
    sums = [send(squares.at[mine], squares.at[mine], s_send.at[q - 1], s_recv.at[q - 1], freq_at(q))
            for q in range(1, 8)]

    slots = nei_ref.shape[0]
    nei = nei_ref[...]
    block = nei >> 8
    hop = ((block - me + (SPAN + count)) & (count - 1)) - SPAN
    slot = jnp.where(hop == SPAN, 2 * SPAN, (block & 7) + jnp.where((block >> 3) != z, SPAN, 0))
    place = slot * (2 * LANES) + (nei & (2 * LANES - 1))
    for half in range(2):
        idx_ref[pl.ds(half, slots, stride=2), :] = place[:, half * LANES:(half + 1) * LANES]
        bins_ref[pl.ds(half, slots, stride=2), :] = bin_ref[:, half * LANES:(half + 1) * LANES]
    idx_ref[2 * slots:, :] = jnp.zeros((TALL - 2 * slots, LANES), jnp.int32)
    bins_ref[2 * slots:, :] = jnp.zeros((TALL - 2 * slots, LANES), jnp.int32)

    small = []
    for q in range(1, 5):
        for c in range(4):
            for w in range(2):
                if q == 4 and w != c // 2:
                    continue
                block_at = lax.rem(y + (8 - q if w == 0 else q), 8)
                turn = lax.div(y - q + 8, 8) if w == 0 else lax.div(y + q, 8)
                if q == 4:
                    turn = lax.div(y + 4, 8)
                flows[w, q - 1, c].wait_recv()
                held = win_ref.at[block_at, chunk(c)]
                if q < 3 or (q == 3 and w == c // 2):
                    flows[w, q, c] = send(held, held, y_send.at[w, q, c], y_recv.at[w, q, c], y_at(ways[w]))
                at = (q - 1) * 2 + w if q < 4 else 6
                rows.append(send(held, win_ref.at[8 + block_at, chunk(c)], z_send.at[at, c], z_recv.at[at, c],
                                 z_at(1 + 6 * turn)))
        if q == 1:
            for copy in sums:
                copy.wait()
            total = squares[0]
            for other in range(1, 8):
                total = total + squares[other]
            packed = total
            for part in range(2):
                for half in range(2):
                    value = v_ref[part:part + 1, half * LANES:(half + 1) * LANES]
                    packed = jnp.where(sub == part * 2 + half, value, packed)
            message[...] = packed
            vwin_ref[y] = packed
            small = [send(message, vwin_ref.at[landing_slot(y, step)], v_send.at[n], v_recv.at[n],
                          img_at(me, step, count)) for n, step in enumerate(STEPS)]
    for copy in small + rows:
        copy.wait()
    for copy in flows.values():
        copy.wait_send()
    own.wait()


def split_exact(value):
    high = value.astype(jnp.bfloat16)
    low = (value - high.astype(jnp.float32)).astype(jnp.bfloat16)
    return jnp.concatenate([high, low], axis=1)


def lane_sums(select, value):
    return lax.dot_general(select, value, (((1,), (1,)), ((), ())), preferred_element_type=jnp.float32)


def pair_part(groups, idx_ref, win_ref, vwin_ref, bins_ref, out_ref, cos_buf, sin_buf, real_buf, imag_buf, root_buf,
              wide, own_tile, turned, places, arrived, tiles):
    rows = win_ref.shape[1]
    eight = lambda group: pl.ds(group * 8 if isinstance(group, int) else pl.multiple_of(group * 8, 8), 8)
    fetch = lambda group, at: pltpu.make_async_copy(idx_ref.at[eight(group)], places[at], arrived.at[at])
    fetch(0, 0).start()
    fetch(1, 1).start()
    first = lax.axis_index("freq") * (LANES // (2 * RADIAL))
    lane = lax.broadcasted_iota(jnp.int32, (8, 2 * LANES), 1)
    sub = lax.broadcasted_iota(jnp.int32, (8, 2 * LANES), 0)
    select = jnp.where((lane % LANES) // (2 * RADIAL) == sub, 1.0, 0.0).astype(jnp.bfloat16)
    freq = (first + lax.broadcasted_iota(jnp.int32, (8, LANES), 0)).astype(jnp.float32)
    line = lax.broadcasted_iota(jnp.int32, (8, LANES), 0)

    for block in range(BLOCKS):
        wide[block * rows:(block + 1) * rows, :] = win_ref[block].astype(jnp.float32)
    here = lax.rem(lax.axis_index("img"), 8)
    own = win_ref[here].astype(jnp.float32)
    own_sq = vwin_ref[here]
    own_root = lax.rsqrt(jnp.where(line % 2 == 0, own_sq[4:5], own_sq[5:6]) + norm_eps)
    own_tile[...] = own
    column = lax.broadcasted_iota(jnp.int32, own.shape, 1)
    turned[...] = jnp.where(column % (2 * RADIAL) < RADIAL,
                            pltpu.roll(own, LANES - RADIAL, 1), -pltpu.roll(own, RADIAL, 1))
    for group in range(groups, 16):
        out_ref[group] = jnp.zeros((8, LANES), jnp.float32)

    def one_group(group, at, then=None):
        fetch(group, at).wait()
        place = places[at]
        for n in range(8):
            for pair in range(LANES):
                tiles[n][pair:pair + 1, :] = wide[pl.ds(place[n, pair], 1), :]
        if then is not None:
            fetch(then, at).start()
        result = jnp.zeros((8, LANES), jnp.float32)
        spots = idx_ref[eight(group), :]
        spins = bins_ref[eight(group), :].astype(jnp.float32)
        ((real, imag, square),) = pick([spots & (LANES - 1)], [spots >> 7], vwin_ref, (0, 2, 4))
        cos, sin = cos_sin_turns(spins)
        cos_buf[group] = cos
        sin_buf[group] = sin
        real_buf[group] = cos * real - sin * imag
        imag_buf[group] = sin * real + cos * imag
        root_buf[group] = lax.rsqrt(square + norm_eps) * own_root
        for n in range(8):
            half = slice((n % 2) * LANES, (n % 2 + 1) * LANES)
            other = tiles[n][...]
            real = split_exact(own_tile[half, :] * other)
            imag = split_exact(turned[half, :] * other)
            sums = lane_sums(select, jnp.concatenate([real, imag], axis=0))
            units = spins[n:n + 1, :] * freq
            cos, sin = cos_sin_turns(units)
            terms = sums[:, :LANES] * cos - sums[:, LANES:] * sin
            result = jnp.where(line == n, jnp.sum(terms, axis=0, keepdims=True), result)
        out_ref[group] = result

    def body(step, carry):
        one_group(2 * step, 0, 2 * step + 2)
        one_group(2 * step + 1, 1, jnp.minimum(2 * step + 3, groups - 1))
        return carry

    lax.fori_loop(0, groups // 2, body, 0)
    one_group(groups - 1, 0)
    fetch(groups - 1, 1).wait()


def pick(low, high, ref, lines):
    found = []
    for where, at in zip(low, high):
        got = [None] * len(lines)
        for row in range(BLOCKS * 2):
            hit = at == row
            for n, line in enumerate(lines):
                first = line + row % 2
                wide = jnp.broadcast_to(ref[row // 2, first:first + 1, :], (8, LANES))
                new = jnp.take_along_axis(wide, where, axis=1, mode="promise_in_bounds")
                got[n] = new if row == 0 else jnp.where(hit, new, got[n])
        found.append(got)
    return found


def fold(total):
    total = total + pltpu.roll(total, 4, 0)
    return total + pltpu.roll(total, 2, 0)


def power_part(count, groups, part_ref, idx_ref, deg_ref, weights_ref, vec_ref,
               cos_buf, sin_buf, real_buf, imag_buf, root_buf, rs_buf, ag_buf, vec1, vec2, ynorm, znorm,
               rs_send, rs_recv, ag_send, ag_recv, v_send, v_recv, n_send, n_recv):
    me = lax.axis_index("img")
    mine = lax.axis_index("freq")
    y, z = lax.rem(me, 8), lax.div(me, 8)
    freq_at = lambda q: {"freq": lax.rem(mine + q, 8)}
    y_at, z_at = ring(me, z, y)
    two = lambda piece: pl.ds(2 * piece, 2)
    copies = []
    for q in range(1, 8):
        copy = pltpu.make_async_remote_copy(
            src_ref=part_ref.at[two(lax.rem(mine + q, 8))], dst_ref=rs_buf.at[q - 1],
            send_sem=rs_send.at[q - 1], recv_sem=rs_recv.at[q - 1], device_id=freq_at(q), device_id_type=MESH)
        copy.start()
        copies.append(copy)
    for copy in copies:
        copy.wait()
    total = part_ref[two(mine)]
    for q in range(7):
        total = total + rs_buf[q]
    ag_buf[two(mine)] = total
    copies = []
    for q in range(1, 8):
        copy = pltpu.make_async_remote_copy(
            src_ref=ag_buf.at[two(mine)], dst_ref=ag_buf.at[two(mine)],
            send_sem=ag_send.at[q - 1], recv_sem=ag_recv.at[q - 1], device_id=freq_at(q), device_id_type=MESH)
        copy.start()
        copies.append(copy)
    for copy in copies:
        copy.wait()

    sub = lax.broadcasted_iota(jnp.int32, (8, LANES), 0)
    degree = jnp.where(sub % 2 == 0, deg_ref[0:1, :], deg_ref[1:2, :])
    low = [idx_ref[m * 8:(m + 1) * 8, :] & (LANES - 1) for m in range(groups)]
    high = [idx_ref[m * 8:(m + 1) * 8, :] >> 7 for m in range(groups)]
    denom = jnp.zeros((8, LANES), jnp.float32)
    for m in range(groups):
        cos_sim = ag_buf[m] * root_buf[m]
        raw = jnp.where((sub // 2 + m * 4) < degree, jnp.exp(sharpness * cos_sim), 0.0)
        weights_ref[m * 8:(m + 1) * 8, :] = raw
        denom = denom + raw
    share = 1.0 / fold(denom)
    for m in range(groups):
        weights_ref[m * 8:(m + 1) * 8, :] = weights_ref[m * 8:(m + 1) * 8, :] * share

    norms = []
    source = None
    for step in range(ITERS):
        real = imag = jnp.zeros((8, LANES), jnp.float32)
        picked = pick(low, high, source, (0, 2)) if step else [None] * groups
        for m, at in enumerate(picked):
            weight = weights_ref[m * 8:(m + 1) * 8, :]
            if step:
                real_at, imag_at = at
                real = real + weight * (cos_buf[m] * real_at - sin_buf[m] * imag_at)
                imag = imag + weight * (sin_buf[m] * real_at + cos_buf[m] * imag_at)
            else:
                real = real + weight * real_buf[m]
                imag = imag + weight * imag_buf[m]
        real, imag = fold(real), fold(imag)
        square = real * real + imag * imag
        norms.append(square + pltpu.roll(square, 1, 0))
        packed = jnp.where(sub % 4 < 2, real, imag)
        if step < ITERS - 1:
            into = (vec1, vec2)[step]
            into[y] = packed
            copies = []
            for n, hop in enumerate(STEPS):
                copy = pltpu.make_async_remote_copy(
                    src_ref=into.at[y], dst_ref=into.at[landing_slot(y, hop)], send_sem=v_send.at[step, n],
                    recv_sem=v_recv.at[step, n], device_id=img_at(me, hop, count), device_id_type=MESH)
                copy.start()
                copies.append(copy)
            for copy in copies:
                copy.wait()
            source = into

    message = jnp.where(sub == 0, norms[0], jnp.where(sub == 1, norms[1], norms[2]))
    for axis, (buf, where) in enumerate(((ynorm, y_at), (znorm, z_at))):
        buf[7] = message
        copies = []
        for q in range(1, 8):
            copy = pltpu.make_async_remote_copy(
                src_ref=buf.at[7], dst_ref=buf.at[q - 1], send_sem=n_send.at[axis, q - 1],
                recv_sem=n_recv.at[axis, q - 1], device_id=where(q), device_id_type=MESH)
            copy.start()
            copies.append(copy)
        for copy in copies:
            copy.wait()
        for q in range(7):
            message = message + buf[q]
    sums = jnp.sum(message, axis=1, keepdims=True)
    images = count * 2 * LANES
    scale = lax.rsqrt(sums[0:1] / images + mean_eps)
    for step in range(1, ITERS):
        scale = scale * lax.rsqrt(scale * scale * sums[step:step + 1] / images + mean_eps)
    vec_ref[...] = packed * scale


def finish_kernel(tall_ref, packed_ref, weights_ref, vec_ref):
    slots = weights_ref.shape[0]
    for half in range(2):
        lanes = slice(half * LANES, (half + 1) * LANES)
        weights_ref[:, lanes] = tall_ref[pl.ds(half, slots, stride=2), :]
        for part in range(2):
            vec_ref[part:part + 1, lanes] = packed_ref[part * 2 + half:part * 2 + half + 1, :]


def whole_call(coef, neighbours, rot_bin, deg, v_init, count):
    rows, width = coef.shape
    groups = TALL // 8
    n = len(STEPS)
    vmem = pl.BlockSpec(memory_space=pltpu.VMEM)
    dma = pltpu.SemaphoreType.DMA
    real = lambda *shape: pltpu.VMEM(shape, jnp.float32)
    window = [pltpu.VMEM((BLOCKS, rows, width), coef.dtype), real(BLOCKS, 8, LANES),
              pltpu.VMEM((TALL, LANES), jnp.int32), pltpu.VMEM((TALL, LANES), jnp.int32),
              real(8, LANES), real(8, 8, LANES), dma((2, 4, 4)), dma((2, 4, 4)), dma((9, 4)), dma((9, 4)),
              dma((n,)), dma((n,)), dma((7,)), dma((7,)), dma((1,))]
    shared = [real(16, 8, LANES)] + [real(groups, 8, LANES)] * 5
    pairs = [real(BLOCKS * rows, width), real(rows, width), real(rows, width), pltpu.SMEM((8, LANES), jnp.int32),
             pltpu.SMEM((8, LANES), jnp.int32), dma((2,))] + [real(LANES, LANES)] * 8
    power = [real(7, 2, 8, LANES), real(16, 8, LANES), real(BLOCKS, 8, LANES), real(BLOCKS, 8, LANES),
             real(8, 8, LANES), real(8, 8, LANES),
             dma((7,)), dma((7,)), dma((7,)), dma((7,)), dma((2, n)), dma((2, n)), dma((2, 7)), dma((2, 7))]

    def kernel(coef_ref, nei_ref, bin_ref, deg_ref, v_ref, weights_ref, vec_ref, *scratch):
        me = lax.axis_index("img")
        mine = lax.axis_index("freq")
        y_at, z_at = ring(me, lax.div(me, 8), lax.rem(me, 8))
        met = greet([img_at(me, step, count) for step in STEPS] + [{"freq": lax.rem(mine + q, 8)} for q in range(1, 8)]
                    + [y_at(q) for q in range(1, 8)] + [z_at(q) for q in range(1, 8)])
        cut = [0]
        for part in (window, shared, pairs, power):
            cut.append(cut[-1] + len(part))
        win, both, pair, last = [scratch[a:b] for a, b in zip(cut, cut[1:])]
        window_part(count, met, coef_ref, nei_ref, bin_ref, v_ref, *win)
        pair_part(groups, win[2], win[0], win[1], win[3], *both, *pair[:3], pair[3:5], pair[5], pair[6:])
        power_part(count, groups, both[0], win[2], deg_ref, weights_ref, vec_ref, *both[1:], *last)

    return pl.pallas_call(
        kernel,
        out_shape=(jax.ShapeDtypeStruct((TALL, LANES), jnp.float32), jax.ShapeDtypeStruct((8, LANES), jnp.float32)),
        in_specs=[vmem] * 5,
        out_specs=(vmem, vmem),
        scratch_shapes=window + shared + pairs + power,
        compiler_params=pltpu.CompilerParams(collective_id=0, has_side_effects=True),
        name="whole",
    )(coef, neighbours, rot_bin, deg, v_init)


def shards(coef, neighbours, rot_bin, degree, v_init):
    count = lax.axis_size("img")
    tall, packed = whole_call(coef, neighbours, rot_bin, degree.reshape(2, LANES), v_init, count)
    vmem = pl.BlockSpec(memory_space=pltpu.VMEM)
    weights, vector = pl.pallas_call(
        finish_kernel,
        out_shape=(jax.ShapeDtypeStruct(neighbours.shape, jnp.float32), jax.ShapeDtypeStruct(v_init.shape, jnp.float32)),
        in_specs=[vmem] * 2,
        out_specs=(vmem, vmem),
        name="finish",
    )(tall, packed)
    return vector, weights


def solution(mesh):
    return jax.shard_map(
        shards,
        mesh=mesh,
        in_specs=(P("img", "freq"), P(None, "img"), P(None, "img"), P("img"), P(None, "img")),
        out_specs=(P(None, "img"), P(None, "img")),
        check_vma=False,
    )
```
